128 devices in a mesh: dp: 4 (over x), expert: 32 (over y, z, core).
Axes of the slice: x: 4, y: 4, z: 4, core: 2. Of those that a mesh axis runs over, the one named last changes fastest.
Arguments:
- hidden: bfloat16 [16384, 2880], P(('dp', 'expert')), may hold values from -12 to 12
- query_base_rows: bfloat16 [16384, 2048], P(('dp', 'expert')), may hold values from -17 to 17
- key_base_rows: bfloat16 [16384, 256], P(('dp', 'expert')), may hold values from -17 to 17
- value_base_rows: bfloat16 [16384, 256], P(('dp', 'expert')), may hold values from -6 to 6
- prompt_number: int32 [4, 4096], P('dp', 'expert'), may hold values from 0 to 15, never falling along the last dimension, each value on 1 to 2048 neighbouring positions
- prompt_adapter: int32 [4, 16], P('dp'), may hold values from 0 to 15
- sinks: float32 [32], replicated, may hold values from 0 to 3
- attention_gain: float32 [2880], replicated, may hold values from 0.5 to 1.5
- adapter_down_factors: bfloat16 [16, 48, 2880], P('dp'), may hold values from -0.109375 to 0.109375
- query_up_factors: bfloat16 [16, 16, 2048], P('dp'), may hold values from -1.5 to 1.5
- key_value_up_factors: bfloat16 [16, 16, 512], P('dp'), may hold values from -1.5 to 1.5
- output_down_factors: bfloat16 [16, 16, 2048], P('dp'), may hold values from -0.125 to 0.125
- output_up_factors: bfloat16 [16, 16, 2880], P('dp'), may hold values from -1.5 to 1.5
- attention_output_weight: bfloat16 [2048, 2880], replicated, may hold values from -0.125 to 0.125
- expert_norm_gain: float32 [2880], replicated, may hold values from 0.5 to 1.5
- expert_gate_up_weight: bfloat16 [32, 1536, 2, 2880], P('expert', 'dp'), may hold values from -0.109375 to 0.109375
- expert_down_weight: bfloat16 [32, 1536, 2880], P('expert', 'dp'), may hold values from -0.15625 to 0.15625
- routes: int32 [16384, 4], P(('dp', 'expert')), may hold values from 0 to 31, all different within a row; in each aligned block of 128 rows (0 to 127, 128 to 255, ...) at most 20 rows name the same one
- routing_gate_weight: float32 [16384, 4], P(('dp', 'expert')), may hold values from 0.05 to 0.5
Outputs:
- layer_out: bfloat16 [16384, 2880], P(('dp', 'expert'))
The draws below stay inside these ranges and needn't reach their ends.
Inputs may be any that keep to these rules, and one draw needn't show every extreme that they name: `routes`: among the rows of one device, no expert is named by more than 20 rows. `prompt_number`: in each request group, prompt numbers never fall along the tokens, and every prompt has at most half of 4096 tokens.
All inputs are finite; a program needn't handle non-finite values.
Results may differ from the reference program's by a relative error of at most 0.0098.
The reference program's roundings to bfloat16 on the way count: a program that leaves them out, or rounds other values in their place, can miss the bound.
Values may be sent and summed in bfloat16 or wider, within the bound.
A program may use at most 256 MiB of HBM per device.

```python
import math
import jax
import jax.numpy as jnp
import numpy as np
from jax import lax

MODEL_DIM = 2880
QH = 32
KVH = 4
HD = 64
ADAPTER_RANK = 16
LIVE_ADAPTERS = 16
FF = 1536
TOP = 4
TOK_DEV = 128
TOKENS = 16384
GROUP_TOK = 4096
DOCS = 16
EXPERTS = 32
CAP = 20
QW = 2048
KW = 256
N_DP = 4


def draw_hidden(key, part):
    first, second, third = jax.random.split(key, 3)
    row_scale = jnp.exp(jax.random.uniform(second, (TOKENS, 1), minval=-1.15, maxval=1.15))
    col_scale = jnp.exp(jax.random.uniform(third, (1, MODEL_DIM), minval=-1.15, maxval=1.15))
    base = jax.random.normal(first, (TOKENS, MODEL_DIM))
    return jnp.clip(base * row_scale * col_scale, -12.0, 12.0).astype(jnp.bfloat16)


def draw_query_base_rows(key, part):
    noise_key = jax.random.fold_in(key, 11)
    groups = QH // KVH
    noise = jnp.clip(jax.random.normal(noise_key, (TOKENS, KVH, groups, HD)), -6.0, 6.0)
    return jnp.clip(noise, -17.0, 17.0).reshape(TOKENS, QH * HD).astype(jnp.bfloat16)


def draw_key_base_rows(key, part):
    noise_key = jax.random.fold_in(key, 13)
    noise = jnp.clip(jax.random.normal(noise_key, (TOKENS, KVH, HD)), -6.0, 6.0)
    return jnp.clip(noise, -17.0, 17.0).reshape(TOKENS, KVH * HD).astype(jnp.bfloat16)


def place_ends(values, own_key, least, top_value):
    longest = values.shape.index(max(values.shape))
    spots = []
    for shift in (0, 1):
        where = [jax.random.randint(jax.random.fold_in(own_key, axis), (), 0, length) for axis, length in enumerate(values.shape)]
        where[longest] = (where[longest] + shift) % values.shape[longest]
        spots.append(tuple(where))
    return values.at[spots[0]].set(least).at[spots[1]].set(top_value)


def shard_levels(key, shape, pieces, low, top_value):
    level = 1.0
    for dim, blocks in pieces:
        heights = jax.random.uniform(jax.random.fold_in(jax.random.fold_in(key, 6), dim), (blocks,), jnp.float32, low / len(pieces), top_value / len(pieces))
        level = level * jnp.repeat(jnp.exp(heights), shape[dim] // blocks).reshape((-1,) + (1,) * (len(shape) - 1 - dim))
    return level


def profile(count, total, bound, slope):
    portions = [(1 << 20) // math.isqrt(standing ** slope) + 1 for standing in range(2, count + 1)]
    surplus, given = total - bound - (count - 1), [1] * (count - 1)
    while surplus > 0:
        free = [i for i in range(count - 1) if given[i] < bound]
        whole, remaining = sum([portions[i] for i in free]), surplus
        for i in free:
            extra = min(bound - given[i], max(1, remaining * portions[i] // whole), surplus)
            given[i] = given[i] + extra
            surplus = surplus - extra
    return np.array([bound] + given)


def ragged_sizes(rng, number_of, total, reach, skew):
    if number_of == 2:
        one = jax.random.randint(rng, (), max(1, total - reach), min(reach, total - 1) + 1)
        return jnp.stack([one, total - one])
    lengths = jnp.asarray(profile(number_of, total, reach, skew), jnp.int32)
    couples = (number_of - 1) // 2
    source_of, receiver = lengths[1:1 + 2 * couples:2], lengths[2:2 + 2 * couples:2]
    slack = jnp.minimum(source_of - 1, reach - receiver)
    moved = jax.random.randint(jax.random.fold_in(rng, 1), (couples,), 0, 1 << 20) % (slack + 1)
    lengths = lengths.at[1:1 + 2 * couples:2].set(source_of - moved).at[2:2 + 2 * couples:2].set(receiver + moved)
    return lengths[jax.random.permutation(jax.random.fold_in(rng, 2), number_of)]


def assign_block(stream_key, own, number, rows, number_of, top, reach, lean):
    ranking = jax.random.permutation(stream_key, number_of)
    heavy_load, usual = portions_of(number_of, rows * top, reach, lean, True), portions_of(number_of, rows * top, reach, lean, False)
    places = jnp.arange(number_of)

    def named(sizes, turn):
        used = int((sizes > 0).sum())
        fixed = max(1, used // 4)
        moved = fixed + (places - fixed + turn * (used - fixed)) % max(1, number_of - fixed)
        return jnp.zeros((number_of,), jnp.int32).at[ranking[jnp.where(places < fixed, places, moved)]].set(jnp.asarray(sizes, jnp.int32))

    sizes = jnp.where(number % 4 == 0, named(heavy_load, number // 4), named(usual, number - number // 4 - 1))
    mixed = jax.random.permutation(jax.random.fold_in(own, 3), number_of)
    donor, receiver = mixed[0:number_of // 2 * 2:2], mixed[1:number_of // 2 * 2:2]
    margin = jnp.minimum(sizes[donor] - 1, reach - sizes[receiver]) // 2
    margin = jnp.where((donor == ranking[0]) | (receiver == ranking[0]) | (sizes[receiver] == 0), 0, jnp.maximum(margin, 0))
    moved = jax.random.randint(jax.random.fold_in(own, 4), (number_of // 2,), 0, 1 << 20) % (margin + 1)
    sizes = sizes.at[donor].add(-moved).at[receiver].add(moved)
    items = jnp.searchsorted(jnp.cumsum(sizes), jnp.arange(rows * top), side="right").astype(jnp.int32)
    table = items.reshape(top, rows).T
    table = table[jax.random.permutation(jax.random.fold_in(own, 1), rows)]
    turn = jax.random.randint(jax.random.fold_in(own, 2), (rows, 1), 0, top)
    return jnp.take_along_axis(table, (jnp.arange(top)[None, :] + turn) % top, axis=1)


def portions_of(count, total, reach, skew, full):
    loads = [(1 << 20) // math.isqrt(standing ** skew) + 1 for standing in range(1, count + 1)]
    largest = reach if full else min(reach, max(-(-total // count), total * loads[0] // sum(loads)))
    least = 1 if total - largest >= count - 1 else 0
    given, rest = [largest] + [least] * (count - 1), total - largest - least * (count - 1)
    while rest > 0:
        free = [i for i in range(1, count) if given[i] < largest] or [i for i in range(1, count) if given[i] < reach]
        pool, left = sum([loads[i] for i in free]), rest
        for i in free:
            more = min(reach - given[i], max(1, left * loads[i] // pool), rest)
            given[i] = given[i] + more
            rest = rest - more
    return np.array(given)


def gaussian(rng, dims, scale, most, pieces=(), kind=jnp.bfloat16):
    values = jax.random.normal(rng, dims, jnp.float32) * scale
    if len(pieces) > 0:
        values = shard_levels(rng, dims, pieces, -0.22, 0.18) * values
    return jnp.clip(values, min=-most, max=most).astype(kind)


def setup_inputs(seed: int = 0) -> dict:
    key_list = jax.random.split(jax.random.key(seed), 20)
    hidden = draw_hidden(jax.random.fold_in(key_list[19], 71), 0)
    query_base_rows = draw_query_base_rows(jax.random.fold_in(key_list[19], 71), 0)
    key_base_rows = draw_key_base_rows(jax.random.fold_in(key_list[19], 71), 0)
    value_base_rows = gaussian(key_list[3], (TOKENS, KW), 1.0, 6.0, ((0, 128),))
    prompt_number = jax.vmap(lambda own: jnp.searchsorted(jnp.cumsum(ragged_sizes(own, DOCS, GROUP_TOK, GROUP_TOK // 2, 2)), jnp.arange(GROUP_TOK), side="right"))(jax.random.split(key_list[4], N_DP)).reshape((N_DP, GROUP_TOK)).astype(jnp.int32)
    prompt_adapter = place_ends(jax.random.randint(key_list[5], (N_DP, DOCS), 0, LIVE_ADAPTERS), jax.random.fold_in(key_list[5], 1), 0, LIVE_ADAPTERS - 1).astype(jnp.int32)
    sinks = jnp.clip(jax.random.uniform(key_list[6], (QH,), jnp.float32, 0.0, 3.0), 0.0, 3.0)
    attention_gain = jnp.clip(1.0 + 0.1 * jax.random.normal(key_list[7], (MODEL_DIM,), jnp.float32), 0.5, 1.5)
    adapter_down_factors = gaussian(key_list[8], (LIVE_ADAPTERS, 3 * ADAPTER_RANK, MODEL_DIM), MODEL_DIM ** -0.5, 0.109375, ((0, 4),))
    query_up_factors = gaussian(key_list[9], (LIVE_ADAPTERS, ADAPTER_RANK, QW), ADAPTER_RANK ** -0.5, 1.5, ((0, 4),))
    key_value_up_factors = gaussian(key_list[10], (LIVE_ADAPTERS, ADAPTER_RANK, 2 * KW), ADAPTER_RANK ** -0.5, 1.5, ((0, 4),))
    output_down_factors = gaussian(key_list[11], (LIVE_ADAPTERS, ADAPTER_RANK, QW), QW ** -0.5, 0.125, ((0, 4),))
    output_up_factors = gaussian(key_list[12], (LIVE_ADAPTERS, ADAPTER_RANK, MODEL_DIM), ADAPTER_RANK ** -0.5, 1.5, ((0, 4),))
    attention_output_weight = gaussian(key_list[13], (QW, MODEL_DIM), QW ** -0.5, 0.125)
    expert_norm_gain = jnp.clip(1.0 + 0.1 * jax.random.normal(key_list[14], (MODEL_DIM,), jnp.float32), 0.5, 1.5)
    expert_gate_up_weight = gaussian(key_list[15], (EXPERTS, FF, 2, MODEL_DIM), MODEL_DIM ** -0.5, 0.109375, ((0, 32), (1, 4)))
    expert_down_weight = gaussian(key_list[16], (EXPERTS, FF, MODEL_DIM), FF ** -0.5, 0.15625, ((0, 32), (1, 4)))
    routes_keys = jax.random.split(jax.random.fold_in(key_list[17], 1), TOKENS // TOK_DEV)
    routes_turns = jax.random.permutation(jax.random.fold_in(key_list[17], 3), TOKENS // TOK_DEV)
    routes = jax.vmap(lambda own, number: assign_block(jax.random.fold_in(key_list[17], 2), own, number, TOK_DEV, EXPERTS, TOP, CAP, 1))(routes_keys, routes_turns).reshape((TOKENS, TOP))
    routing_gate_weight = jnp.clip(0.05 + 0.45 * jax.random.uniform(key_list[18], (TOKENS, TOP), jnp.float32) ** shard_levels(key_list[18], (TOKENS, TOP), ((0, 128),), -0.2, 0.2), 0.05, 0.5)
    return {"hidden": hidden, "query_base_rows": query_base_rows, "key_base_rows": key_base_rows, "value_base_rows": value_base_rows, "prompt_number": prompt_number, "prompt_adapter": prompt_adapter, "sinks": sinks, "attention_gain": attention_gain, "adapter_down_factors": adapter_down_factors, "query_up_factors": query_up_factors, "key_value_up_factors": key_value_up_factors, "output_down_factors": output_down_factors, "output_up_factors": output_up_factors, "attention_output_weight": attention_output_weight, "expert_norm_gain": expert_norm_gain, "expert_gate_up_weight": expert_gate_up_weight, "expert_down_weight": expert_down_weight, "routes": routes, "routing_gate_weight": routing_gate_weight}


EPSILON = 1e-05
ROPE_BASE = 150000.0
SCORE_SCALE = 0.125
NEGATIVE = -1e+30

def rms_scale(rows_in, gain):
    floats = rows_in.astype(jnp.float32)
    mean_square = lax.optimization_barrier(jnp.mean(floats * floats, axis=-1, keepdims=True))
    return (floats * lax.rsqrt(mean_square + EPSILON) * gain).astype(jnp.bfloat16)

def rotate(heads, positions):
    head_dim = heads.shape[-1]
    half = head_dim // 2
    freqs = ROPE_BASE ** (-(2.0 * jnp.arange(half, dtype=jnp.float32) / head_dim))
    angle = positions.astype(jnp.float32)[:, None] * freqs[None, :]
    cosine = jnp.cos(angle)[:, None, :]
    sine = jnp.sin(angle)[:, None, :]
    first = heads[..., :half]
    second = heads[..., half:]
    return jnp.concatenate([first * cosine - second * sine, second * cosine + first * sine], axis=-1)

def multiply_rows(left, right):
    return lax.dot_general(left, right, (((1,), (1,)), ((), ())), preferred_element_type=jnp.float32)

def select_adapter(all_terms, adapter_selector, span):
    stacked = all_terms.reshape(all_terms.shape[0], adapter_selector.shape[1], span)
    return lax.optimization_barrier(jnp.sum(stacked * adapter_selector[:, :, None], axis=1))

def spread(adapter_selector, low_part):
    joined = adapter_selector[:, :, None] * low_part.astype(jnp.float32)[:, None, :]
    return joined.reshape(joined.shape[0], -1).astype(jnp.bfloat16)

def round_trip(floats):
    return lax.optimization_barrier(floats.astype(jnp.bfloat16)).astype(jnp.float32)

def expert_out(rows_in, gate_up, down_rows):
    gate_out = multiply_rows(rows_in, gate_up[:, 0, :])
    up_out = multiply_rows(rows_in, gate_up[:, 1, :])
    activation = (jax.nn.silu(gate_out) * up_out).astype(jnp.bfloat16)
    block_units = FF // N_DP
    summed = jnp.zeros((rows_in.shape[0], down_rows.shape[1]), jnp.float32)
    for quarter in range(N_DP):
        part_act = activation[:, quarter * block_units:(quarter + 1) * block_units]
        part_down = down_rows[quarter * block_units:(quarter + 1) * block_units]
        summed = summed + round_trip(jnp.dot(part_act, part_down, preferred_element_type=jnp.float32))
    return summed.astype(jnp.bfloat16)

def reference(hidden, query_base_rows, key_base_rows, value_base_rows, prompt_number, prompt_adapter, sinks, attention_gain, adapter_down_factors, query_up_factors, key_value_up_factors, output_down_factors, output_up_factors, attention_output_weight, expert_norm_gain, expert_gate_up_weight, expert_down_weight, routes, routing_gate_weight):
    tokens = hidden.shape[0]
    group = tokens // N_DP
    doc_count = prompt_adapter.shape[1]
    adapter_table = adapter_down_factors.shape[0]
    q_width = query_base_rows.shape[1]
    kv_width = key_base_rows.shape[1]
    kv_heads = kv_width // HD
    groups = QH // kv_heads
    doc_range = jnp.arange(doc_count, dtype=jnp.int32)
    doc_hot = (prompt_number[:, :, None] == doc_range[None, None, :]).astype(jnp.int32)
    counts = lax.optimization_barrier(jnp.sum(doc_hot, axis=1))
    firsts = jnp.cumsum(counts, axis=1) - counts
    starts = lax.optimization_barrier(jnp.sum(doc_hot * firsts[:, None, :], axis=2))
    positions = (jnp.arange(group, dtype=jnp.int32)[None, :] - starts).reshape(tokens)
    adapter_of = lax.optimization_barrier(jnp.sum(doc_hot * prompt_adapter[:, None, :], axis=2)).reshape(tokens)
    adapter_selector = (adapter_of[:, None] == jnp.arange(adapter_table, dtype=jnp.int32)[None, :]).astype(jnp.float32)
    normalized_tokens = rms_scale(hidden, attention_gain)
    lowrank_part = select_adapter(multiply_rows(normalized_tokens, adapter_down_factors.reshape(adapter_table * 3 * ADAPTER_RANK, MODEL_DIM)), adapter_selector, 3 * ADAPTER_RANK).astype(jnp.bfloat16)
    q_delta = jnp.dot(spread(adapter_selector, lowrank_part[:, :ADAPTER_RANK]), query_up_factors.reshape(adapter_table * ADAPTER_RANK, q_width), preferred_element_type=jnp.float32)
    k_delta = jnp.dot(spread(adapter_selector, lowrank_part[:, ADAPTER_RANK:2 * ADAPTER_RANK]), key_value_up_factors[:, :, :kv_width].reshape(adapter_table * ADAPTER_RANK, kv_width), preferred_element_type=jnp.float32)
    v_delta = jnp.dot(spread(adapter_selector, lowrank_part[:, 2 * ADAPTER_RANK:]), key_value_up_factors[:, :, kv_width:].reshape(adapter_table * ADAPTER_RANK, kv_width), preferred_element_type=jnp.float32)
    queries = rotate((query_base_rows.astype(jnp.float32) + q_delta).reshape(tokens, QH, HD), positions)
    queries = lax.optimization_barrier(queries.astype(jnp.bfloat16))
    key_rows = rotate((key_base_rows.astype(jnp.float32) + k_delta).reshape(tokens, kv_heads, HD), positions)
    key_rows = lax.optimization_barrier(key_rows.astype(jnp.bfloat16))
    value_rows = lax.optimization_barrier((value_base_rows.astype(jnp.float32) + v_delta).astype(jnp.bfloat16)).reshape(tokens, kv_heads, HD)
    sink_grid = sinks.reshape(kv_heads, groups)
    block_rows = 512
    key_index = jnp.arange(group, dtype=jnp.int32)

    def attend_group(group_index):
        group_q = lax.dynamic_slice_in_dim(queries, group_index * group, group, 0).reshape(group // block_rows, block_rows, kv_heads, groups, HD)
        group_k = lax.dynamic_slice_in_dim(key_rows, group_index * group, group, 0).astype(jnp.float32)
        group_v = lax.dynamic_slice_in_dim(value_rows, group_index * group, group, 0).astype(jnp.float32)
        group_ids = lax.dynamic_index_in_dim(prompt_number, group_index, 0, keepdims=False)

        def attend_block(block_args):
            block_index, block_q = block_args
            query_index = block_index * block_rows + jnp.arange(block_rows, dtype=jnp.int32)
            query_ids = lax.dynamic_slice_in_dim(group_ids, block_index * block_rows, block_rows, 0)
            scores = jnp.einsum('tkgd,nkd->kgtn', block_q.astype(jnp.float32), group_k) * SCORE_SCALE
            allowed = (key_index[None, :] <= query_index[:, None]) & (group_ids[None, :] == query_ids[:, None])
            scores = jnp.where(allowed[None, None], scores, NEGATIVE)
            running_max = jnp.maximum(lax.optimization_barrier(jnp.max(scores, axis=-1)), sink_grid[:, :, None])
            exps = jnp.exp(scores - running_max[..., None])
            running_sum = lax.optimization_barrier(jnp.sum(exps, axis=-1)) + jnp.exp(sink_grid[:, :, None] - running_max)
            weighted = jnp.einsum('kgtn,nkd->kgtd', round_trip(exps), group_v)
            result = weighted / running_sum[..., None]
            return jnp.transpose(result, (2, 0, 1, 3)).astype(jnp.bfloat16)
        outs = lax.map(attend_block, (jnp.arange(group // block_rows, dtype=jnp.int32), group_q))
        return outs.reshape(group, q_width)
    attended = lax.map(attend_group, jnp.arange(N_DP, dtype=jnp.int32)).reshape(tokens, q_width)
    o_low = select_adapter(multiply_rows(attended, output_down_factors.reshape(adapter_table * ADAPTER_RANK, q_width)), adapter_selector, ADAPTER_RANK).astype(jnp.bfloat16)
    projected = jnp.dot(attended, attention_output_weight, preferred_element_type=jnp.float32)
    projected = projected + jnp.dot(spread(adapter_selector, o_low), output_up_factors.reshape(adapter_table * ADAPTER_RANK, MODEL_DIM), preferred_element_type=jnp.float32)
    mid = (hidden.astype(jnp.float32) + projected).astype(jnp.bfloat16)
    moe_in = rms_scale(mid, expert_norm_gain)
    experts = expert_gate_up_weight.shape[0]
    devices = tokens // TOK_DEV
    capacity = 5 * TOK_DEV * TOP // (4 * experts)
    flat_routes = routes.reshape(devices, TOK_DEV * TOP)
    route_hot = (flat_routes[:, :, None] == jnp.arange(experts, dtype=jnp.int32)[None, None, :]).astype(jnp.int32)
    before = jnp.cumsum(route_hot, axis=1) - route_hot
    slot_index = lax.optimization_barrier(jnp.sum(before * route_hot, axis=2))
    buffer_index = flat_routes * capacity + slot_index
    device_range = jnp.arange(devices, dtype=jnp.int32)
    source = jnp.full((devices, experts * capacity), -1, jnp.int32)
    source = source.at[device_range[:, None], buffer_index].set(jnp.arange(TOK_DEV * TOP, dtype=jnp.int32)[None, :])
    filled = source >= 0
    token_of = jnp.maximum(source, 0) // TOP + device_range[:, None] * TOK_DEV
    token_of = jnp.transpose(token_of.reshape(devices, experts, capacity), (1, 0, 2)).reshape(experts, devices * capacity)
    filled = jnp.transpose(filled.reshape(devices, experts, capacity), (1, 0, 2)).reshape(experts, devices * capacity)

    def run_expert(expert_args):
        gate_up, down_rows, take_rows, keep_rows = expert_args
        picked = jnp.take(moe_in, take_rows, axis=0)
        picked = jnp.where(keep_rows[:, None], picked, jnp.zeros_like(picked))
        return expert_out(picked, gate_up, down_rows)
    results = lax.map(run_expert, (expert_gate_up_weight, expert_down_weight, token_of, filled)).reshape(experts, devices, capacity, MODEL_DIM)
    device_of = jnp.broadcast_to(device_range[:, None], (devices, TOK_DEV * TOP)).reshape(tokens * TOP)
    chosen = results[flat_routes.reshape(tokens * TOP), device_of, slot_index.reshape(tokens * TOP)]
    scaled = chosen.astype(jnp.float32) * routing_gate_weight.reshape(tokens * TOP)[:, None]
    moe = lax.optimization_barrier(jnp.sum(scaled.reshape(tokens, TOP, MODEL_DIM), axis=1))
    return (mid.astype(jnp.float32) + moe).astype(jnp.bfloat16)
```

```python
import jax
import jax.numpy as jnp
from jax import lax
from jax.sharding import PartitionSpec as P

HD = 64
ADAPTER_RANK = 16
TOP = 4


EPSILON = 1e-05
ROPE_BASE = 150000.0
SCORE_SCALE = 0.125
NEGATIVE = -1e30


def rms_scale(rows_in, gain):
    floats = rows_in.astype(jnp.float32)
    mean_square = jnp.mean(floats * floats, axis=-1, keepdims=True)
    return (floats * lax.rsqrt(mean_square + EPSILON) * gain).astype(jnp.bfloat16)


def rotate(heads, positions):
    head_dim = heads.shape[-1]
    half = head_dim // 2
    freqs = ROPE_BASE ** (-(2.0 * jnp.arange(half, dtype=jnp.float32) / head_dim))
    angle = positions.astype(jnp.float32)[:, None] * freqs[None, :]
    cosine = jnp.cos(angle)[:, None, :]
    sine = jnp.sin(angle)[:, None, :]
    first = heads[..., :half]
    second = heads[..., half:]
    return jnp.concatenate(
        [first * cosine - second * sine, second * cosine + first * sine], axis=-1
    )


def multiply_rows(left, right):
    return lax.dot_general(
        left, right, (((1,), (1,)), ((), ())), preferred_element_type=jnp.float32
    )


def select_adapter(all_terms, adapter_selector, span):
    stacked = all_terms.reshape(all_terms.shape[0], adapter_selector.shape[1], span)
    return jnp.sum(stacked * adapter_selector[:, :, None], axis=1)


def spread(adapter_selector, low_part):
    joined = adapter_selector[:, :, None] * low_part.astype(jnp.float32)[:, None, :]
    return joined.reshape(joined.shape[0], -1).astype(jnp.bfloat16)


def expert_hidden(rows_in, gate_up):
    gate_out = multiply_rows(rows_in, gate_up[:, 0, :])
    up_out = multiply_rows(rows_in, gate_up[:, 1, :])
    return (jax.nn.silu(gate_out) * up_out).astype(jnp.bfloat16)


def shards(
    hidden,
    query_base_rows,
    key_base_rows,
    value_base_rows,
    prompt_number,
    prompt_adapter,
    sinks,
    attention_gain,
    adapter_down_factors,
    query_up_factors,
    key_value_up_factors,
    output_down_factors,
    output_up_factors,
    attention_output_weight,
    expert_norm_gain,
    expert_gate_up_weight,
    expert_down_weight,
    routes,
    routing_gate_weight,
):
    tok_rows = hidden.shape[0]
    model_width = hidden.shape[1]
    q_width = query_base_rows.shape[1]
    kv_width = key_base_rows.shape[1]
    kv_heads = kv_width // HD
    groups = q_width // HD // kv_heads
    doc_count = prompt_adapter.shape[1]
    row_ids = lax.all_gather(prompt_number, "expert", axis=1, tiled=True)[0]
    my_ids = prompt_number[0]
    doc_range = jnp.arange(doc_count, dtype=jnp.int32)
    counts = jnp.sum((row_ids[:, None] == doc_range[None, :]).astype(jnp.int32), axis=0)
    firsts = jnp.cumsum(counts) - counts
    doc_hot = (my_ids[:, None] == doc_range[None, :]).astype(jnp.int32)
    query_index = lax.axis_index("expert") * tok_rows + jnp.arange(tok_rows, dtype=jnp.int32)
    positions = query_index - jnp.sum(doc_hot * firsts[None, :], axis=1)
    adapter_of = jnp.sum(doc_hot * prompt_adapter[0][None, :], axis=1)
    local_factors = (
        adapter_down_factors,
        query_up_factors,
        key_value_up_factors,
        output_down_factors,
        output_up_factors,
    )
    local_count = adapter_down_factors.shape[0]
    joined_factors = jnp.concatenate([f.reshape(local_count, -1) for f in local_factors], axis=1)
    all_factors = lax.all_gather(joined_factors, "dp", axis=0, tiled=True)
    factors = []
    offset = 0
    for f in local_factors:
        width = f.shape[1] * f.shape[2]
        factors.append(
            all_factors[:, offset : offset + width].reshape(all_factors.shape[0], f.shape[1], f.shape[2])
        )
        offset += width
    all_down, all_up_query, all_up_keyval, all_o_down, all_o_up = factors
    adapter_table = all_down.shape[0]
    adapter_selector = (
        adapter_of[:, None] == jnp.arange(adapter_table, dtype=jnp.int32)[None, :]
    ).astype(jnp.float32)
    normalized_tokens = rms_scale(hidden, attention_gain)
    lowrank_part = select_adapter(
        multiply_rows(
            normalized_tokens, all_down.reshape(adapter_table * 3 * ADAPTER_RANK, model_width)
        ),
        adapter_selector,
        3 * ADAPTER_RANK,
    ).astype(jnp.bfloat16)
    q_delta = jnp.dot(
        spread(adapter_selector, lowrank_part[:, :ADAPTER_RANK]),
        all_up_query.reshape(adapter_table * ADAPTER_RANK, q_width),
        preferred_element_type=jnp.float32,
    )
    k_delta = jnp.dot(
        spread(adapter_selector, lowrank_part[:, ADAPTER_RANK : 2 * ADAPTER_RANK]),
        all_up_keyval[:, :, :kv_width].reshape(adapter_table * ADAPTER_RANK, kv_width),
        preferred_element_type=jnp.float32,
    )
    v_delta = jnp.dot(
        spread(adapter_selector, lowrank_part[:, 2 * ADAPTER_RANK :]),
        all_up_keyval[:, :, kv_width:].reshape(adapter_table * ADAPTER_RANK, kv_width),
        preferred_element_type=jnp.float32,
    )
    queries = rotate(
        (query_base_rows.astype(jnp.float32) + q_delta).reshape(tok_rows, kv_heads * groups, HD),
        positions,
    )
    queries = queries.astype(jnp.bfloat16).reshape(tok_rows, kv_heads, groups, HD)
    key_rows = rotate(
        (key_base_rows.astype(jnp.float32) + k_delta).reshape(tok_rows, kv_heads, HD), positions
    )
    key_rows = key_rows.astype(jnp.bfloat16).reshape(tok_rows, kv_width)
    value_rows = (value_base_rows.astype(jnp.float32) + v_delta).astype(jnp.bfloat16)
    sink_grid = sinks.reshape(kv_heads, groups)
    running_max = jnp.broadcast_to(sink_grid[:, :, None], (kv_heads, groups, tok_rows))
    running_sum = jnp.ones((kv_heads, groups, tok_rows), jnp.float32)
    weighted = jnp.zeros((kv_heads, groups, tok_rows, HD), jnp.float32)
    piece_kv = lax.all_gather(
        jnp.concatenate([key_rows, value_rows], axis=1), "expert", axis=0, tiled=True
    )
    piece_rows = piece_kv.shape[0]
    piece_keys = piece_kv[:, :kv_width].reshape(piece_rows, kv_heads, HD)
    piece_values = piece_kv[:, kv_width:].reshape(piece_rows, kv_heads, HD)
    gate_up_local = jnp.transpose(expert_gate_up_weight[0], (1, 0, 2))
    gate_up_local, down_local, _ = lax.optimization_barrier(
        (gate_up_local, expert_down_weight[0], piece_kv)
    )
    gate_up_full = lax.all_gather(gate_up_local, "dp", axis=1, tiled=True)
    down_full = lax.all_gather(down_local, "dp", axis=0, tiled=True)
    key_index = jnp.arange(piece_rows, dtype=jnp.int32)
    scores = (
        jnp.einsum("tkgd,nkd->kgtn", queries, piece_keys, preferred_element_type=jnp.float32)
        * SCORE_SCALE
    )
    allowed = (key_index[None, :] <= query_index[:, None]) & (row_ids[None, :] == my_ids[:, None])
    scores = jnp.where(allowed[None, None], scores, NEGATIVE)
    fresh_max = jnp.maximum(running_max, jnp.max(scores, axis=-1))
    exps = jnp.exp(scores - fresh_max[..., None])
    factor = jnp.exp(running_max - fresh_max)
    running_sum = running_sum * factor + jnp.sum(exps, axis=-1)
    weighted = weighted * factor[..., None] + jnp.einsum(
        "kgtn,nkd->kgtd",
        exps.astype(jnp.bfloat16),
        piece_values,
        preferred_element_type=jnp.float32,
    )
    attended = (
        jnp.transpose(weighted / running_sum[..., None], (2, 0, 1, 3))
        .reshape(tok_rows, q_width)
        .astype(jnp.bfloat16)
    )
    o_low = select_adapter(
        multiply_rows(attended, all_o_down.reshape(adapter_table * ADAPTER_RANK, q_width)),
        adapter_selector,
        ADAPTER_RANK,
    ).astype(jnp.bfloat16)
    projected = jnp.dot(attended, attention_output_weight, preferred_element_type=jnp.float32)
    projected = projected + jnp.dot(
        spread(adapter_selector, o_low),
        all_o_up.reshape(adapter_table * ADAPTER_RANK, model_width),
        preferred_element_type=jnp.float32,
    )
    mid = (hidden.astype(jnp.float32) + projected).astype(jnp.bfloat16)
    moe_in = rms_scale(mid, expert_norm_gain)
    exp_dev = expert_gate_up_weight.shape[0]
    experts = lax.axis_size("expert") * exp_dev
    capacity = 5 * tok_rows * TOP // (4 * experts)
    flat_routes = routes.reshape(tok_rows * TOP)
    route_hot = (flat_routes[:, None] == jnp.arange(experts, dtype=jnp.int32)[None, :]).astype(
        jnp.int32
    )
    before = jnp.cumsum(route_hot, axis=0) - route_hot
    slot_index = jnp.sum(before * route_hot, axis=1)
    buffer_index = flat_routes * capacity + slot_index
    source = (
        jnp.full((experts * capacity,), -1, jnp.int32)
        .at[buffer_index]
        .set(jnp.arange(tok_rows * TOP, dtype=jnp.int32))
    )
    filled = source >= 0
    picked = jnp.take(moe_in, jnp.maximum(source, 0) // TOP, axis=0)
    dispatch = jnp.where(filled[:, None], picked, jnp.zeros_like(picked)).reshape(
        experts, capacity, model_width
    )
    arrived = lax.all_to_all(dispatch, "expert", split_axis=0, concat_axis=0, tiled=True)
    flat_rows = arrived.reshape(-1, model_width)
    gate_out = multiply_rows(flat_rows, gate_up_full[0])
    up_out = multiply_rows(flat_rows, gate_up_full[1])
    activation = (jax.nn.silu(gate_out) * up_out).astype(jnp.bfloat16)
    block_units = expert_gate_up_weight.shape[1]
    block_count = down_full.shape[0] // block_units
    summed = jnp.zeros((flat_rows.shape[0], model_width), jnp.float32)
    for quarter in range(block_count):
        part = jnp.dot(
            activation[:, quarter * block_units : (quarter + 1) * block_units],
            down_full[quarter * block_units : (quarter + 1) * block_units],
            preferred_element_type=jnp.float32,
        )
        summed = summed + part.astype(jnp.bfloat16).astype(jnp.float32)
    expert_rows = summed.astype(jnp.bfloat16).reshape(arrived.shape)
    returned = lax.all_to_all(expert_rows, "expert", split_axis=0, concat_axis=0, tiled=True)
    chosen = jnp.take(returned.reshape(experts * capacity, model_width), buffer_index, axis=0)
    scaled = chosen.astype(jnp.float32) * routing_gate_weight.reshape(tok_rows * TOP)[:, None]
    moe = jnp.sum(scaled.reshape(tok_rows, TOP, model_width), axis=1)
    return (mid.astype(jnp.float32) + moe).astype(jnp.bfloat16)


def solution(mesh):
    placed = (
        P(("dp", "expert"), None),
        P(("dp", "expert"), None),
        P(("dp", "expert"), None),
        P(("dp", "expert"), None),
        P("dp", "expert"),
        P("dp", None),
        P(),
        P(),
        P("dp", None, None),
        P("dp", None, None),
        P("dp", None, None),
        P("dp", None, None),
        P("dp", None, None),
        P(),
        P(),
        P("expert", "dp", None, None),
        P("expert", "dp", None),
        P(("dp", "expert"), None),
        P(("dp", "expert"), None),
    )
    return jax.shard_map(
        shards, mesh=mesh, in_specs=placed, out_specs=P(("dp", "expert"), None), check_vma=False
    )
```

```python
import jax
import jax.numpy as jnp
from jax import lax
from jax.sharding import PartitionSpec as P

HD = 64
ADAPTER_RANK = 16
TOP = 4


EPSILON = 1e-05
ROPE_BASE = 150000.0
SCORE_SCALE = 0.125
NEGATIVE = -1e30


def rms_scale(rows_in, gain):
    floats = rows_in.astype(jnp.float32)
    mean_square = jnp.mean(floats * floats, axis=-1, keepdims=True)
    return (floats * lax.rsqrt(mean_square + EPSILON) * gain).astype(jnp.bfloat16)


def rotate(heads, positions):
    head_dim = heads.shape[-1]
    half = head_dim // 2
    freqs = ROPE_BASE ** (-(2.0 * jnp.arange(half, dtype=jnp.float32) / head_dim))
    angle = positions.astype(jnp.float32)[:, None] * freqs[None, :]
    cosine = jnp.cos(angle)[:, None, :]
    sine = jnp.sin(angle)[:, None, :]
    first = heads[..., :half]
    second = heads[..., half:]
    return jnp.concatenate(
        [first * cosine - second * sine, second * cosine + first * sine], axis=-1
    )


def multiply_rows(left, right):
    return lax.dot_general(
        left, right, (((1,), (1,)), ((), ())), preferred_element_type=jnp.float32
    )


def select_adapter(all_terms, adapter_selector, span):
    stacked = all_terms.reshape(all_terms.shape[0], adapter_selector.shape[1], span)
    return jnp.sum(stacked * adapter_selector[:, :, None], axis=1)


def spread(adapter_selector, low_part):
    joined = adapter_selector[:, :, None] * low_part.astype(jnp.float32)[:, None, :]
    return joined.reshape(joined.shape[0], -1).astype(jnp.bfloat16)


def expert_hidden(rows_in, gate_up):
    gate_out = multiply_rows(rows_in, gate_up[:, 0, :])
    up_out = multiply_rows(rows_in, gate_up[:, 1, :])
    return (jax.nn.silu(gate_out) * up_out).astype(jnp.bfloat16)


def shards(
    hidden,
    query_base_rows,
    key_base_rows,
    value_base_rows,
    prompt_number,
    prompt_adapter,
    sinks,
    attention_gain,
    adapter_down_factors,
    query_up_factors,
    key_value_up_factors,
    output_down_factors,
    output_up_factors,
    attention_output_weight,
    expert_norm_gain,
    expert_gate_up_weight,
    expert_down_weight,
    routes,
    routing_gate_weight,
):
    tok_rows = hidden.shape[0]
    model_width = hidden.shape[1]
    q_width = query_base_rows.shape[1]
    kv_width = key_base_rows.shape[1]
    kv_heads = kv_width // HD
    groups = q_width // HD // kv_heads
    doc_count = prompt_adapter.shape[1]
    row_ids = lax.all_gather(prompt_number, "expert", axis=1, tiled=True)[0]
    my_ids = prompt_number[0]
    doc_range = jnp.arange(doc_count, dtype=jnp.int32)
    counts = jnp.sum((row_ids[:, None] == doc_range[None, :]).astype(jnp.int32), axis=0)
    firsts = jnp.cumsum(counts) - counts
    doc_hot = (my_ids[:, None] == doc_range[None, :]).astype(jnp.int32)
    query_index = lax.axis_index("expert") * tok_rows + jnp.arange(tok_rows, dtype=jnp.int32)
    positions = query_index - jnp.sum(doc_hot * firsts[None, :], axis=1)
    adapter_of = jnp.sum(doc_hot * prompt_adapter[0][None, :], axis=1)
    local_factors = (
        adapter_down_factors,
        query_up_factors,
        key_value_up_factors,
        output_down_factors,
        output_up_factors,
    )
    local_count = adapter_down_factors.shape[0]
    joined_factors = jnp.concatenate([f.reshape(local_count, -1) for f in local_factors], axis=1)
    all_factors = lax.all_gather(joined_factors, "dp", axis=0, tiled=True)
    factors = []
    offset = 0
    for f in local_factors:
        width = f.shape[1] * f.shape[2]
        factors.append(
            all_factors[:, offset : offset + width].reshape(all_factors.shape[0], f.shape[1], f.shape[2])
        )
        offset += width
    all_down, all_up_query, all_up_keyval, all_o_down, all_o_up = factors
    adapter_table = all_down.shape[0]
    adapter_selector = (
        adapter_of[:, None] == jnp.arange(adapter_table, dtype=jnp.int32)[None, :]
    ).astype(jnp.float32)
    normalized_tokens = rms_scale(hidden, attention_gain)
    lowrank_part = select_adapter(
        multiply_rows(
            normalized_tokens, all_down.reshape(adapter_table * 3 * ADAPTER_RANK, model_width)
        ),
        adapter_selector,
        3 * ADAPTER_RANK,
    ).astype(jnp.bfloat16)
    q_delta = jnp.dot(
        spread(adapter_selector, lowrank_part[:, :ADAPTER_RANK]),
        all_up_query.reshape(adapter_table * ADAPTER_RANK, q_width),
        preferred_element_type=jnp.float32,
    )
    k_delta = jnp.dot(
        spread(adapter_selector, lowrank_part[:, ADAPTER_RANK : 2 * ADAPTER_RANK]),
        all_up_keyval[:, :, :kv_width].reshape(adapter_table * ADAPTER_RANK, kv_width),
        preferred_element_type=jnp.float32,
    )
    v_delta = jnp.dot(
        spread(adapter_selector, lowrank_part[:, 2 * ADAPTER_RANK :]),
        all_up_keyval[:, :, kv_width:].reshape(adapter_table * ADAPTER_RANK, kv_width),
        preferred_element_type=jnp.float32,
    )
    queries = rotate(
        (query_base_rows.astype(jnp.float32) + q_delta).reshape(tok_rows, kv_heads * groups, HD),
        positions,
    )
    queries = queries.astype(jnp.bfloat16).reshape(tok_rows, kv_heads, groups, HD)
    key_rows = rotate(
        (key_base_rows.astype(jnp.float32) + k_delta).reshape(tok_rows, kv_heads, HD), positions
    )
    key_rows = key_rows.astype(jnp.bfloat16).reshape(tok_rows, kv_width)
    value_rows = (value_base_rows.astype(jnp.float32) + v_delta).astype(jnp.bfloat16)
    sink_grid = sinks.reshape(kv_heads, groups)
    running_max = jnp.broadcast_to(sink_grid[:, :, None], (kv_heads, groups, tok_rows))
    running_sum = jnp.ones((kv_heads, groups, tok_rows), jnp.float32)
    weighted = jnp.zeros((kv_heads, groups, tok_rows, HD), jnp.float32)
    piece_kv = lax.all_gather(
        jnp.concatenate([key_rows, value_rows], axis=1), "expert", axis=0, tiled=True
    )
    piece_rows = piece_kv.shape[0]
    piece_keys = piece_kv[:, :kv_width].reshape(piece_rows, kv_heads, HD)
    piece_values = piece_kv[:, kv_width:].reshape(piece_rows, kv_heads, HD)
    gate_up_local = jnp.transpose(expert_gate_up_weight[0], (1, 0, 2))
    gate_up_local, down_local, _ = lax.optimization_barrier(
        (gate_up_local, expert_down_weight[0], piece_kv)
    )
    gate_up_full = lax.all_gather(gate_up_local, "dp", axis=1, tiled=True)
    down_full = lax.all_gather(down_local, "dp", axis=0, tiled=True)
    window = min(piece_rows, piece_rows // 2 + tok_rows)
    window_start = jnp.clip(
        (lax.axis_index("expert") + 1) * tok_rows - window, 0, piece_rows - window
    )
    piece_keys = lax.dynamic_slice_in_dim(piece_keys, window_start, window, 0)
    piece_values = lax.dynamic_slice_in_dim(piece_values, window_start, window, 0)
    window_ids = lax.dynamic_slice_in_dim(row_ids, window_start, window, 0)
    key_index = window_start + jnp.arange(window, dtype=jnp.int32)
    scores = (
        jnp.einsum("tkgd,nkd->kgtn", queries, piece_keys, preferred_element_type=jnp.float32)
        * SCORE_SCALE
    )
    allowed = (key_index[None, :] <= query_index[:, None]) & (
        window_ids[None, :] == my_ids[:, None]
    )
    scores = jnp.where(allowed[None, None], scores, NEGATIVE)
    fresh_max = jnp.maximum(running_max, jnp.max(scores, axis=-1))
    exps = jnp.exp(scores - fresh_max[..., None])
    factor = jnp.exp(running_max - fresh_max)
    running_sum = running_sum * factor + jnp.sum(exps, axis=-1)
    weighted = weighted * factor[..., None] + jnp.einsum(
        "kgtn,nkd->kgtd",
        exps.astype(jnp.bfloat16),
        piece_values,
        preferred_element_type=jnp.float32,
    )
    attended = (
        jnp.transpose(weighted / running_sum[..., None], (2, 0, 1, 3))
        .reshape(tok_rows, q_width)
        .astype(jnp.bfloat16)
    )
    o_low = select_adapter(
        multiply_rows(attended, all_o_down.reshape(adapter_table * ADAPTER_RANK, q_width)),
        adapter_selector,
        ADAPTER_RANK,
    ).astype(jnp.bfloat16)
    projected = jnp.dot(attended, attention_output_weight, preferred_element_type=jnp.float32)
    projected = projected + jnp.dot(
        spread(adapter_selector, o_low),
        all_o_up.reshape(adapter_table * ADAPTER_RANK, model_width),
        preferred_element_type=jnp.float32,
    )
    mid = (hidden.astype(jnp.float32) + projected).astype(jnp.bfloat16)
    moe_in = rms_scale(mid, expert_norm_gain)
    exp_dev = expert_gate_up_weight.shape[0]
    experts = lax.axis_size("expert") * exp_dev
    capacity = 5 * tok_rows * TOP // (4 * experts)
    flat_routes = routes.reshape(tok_rows * TOP)
    route_hot = (flat_routes[:, None] == jnp.arange(experts, dtype=jnp.int32)[None, :]).astype(
        jnp.int32
    )
    before = jnp.cumsum(route_hot, axis=0) - route_hot
    slot_index = jnp.sum(before * route_hot, axis=1)
    slot_hot = (
        slot_index[:, None] == jnp.arange(capacity, dtype=jnp.int32)[None, :]
    ).astype(jnp.float32)
    pair_hot = route_hot.astype(jnp.float32)[:, :, None] * slot_hot[:, None, :]
    pair_hot = pair_hot.reshape(tok_rows, TOP, experts, capacity)
    dispatch_hot = jnp.sum(pair_hot, axis=1).astype(jnp.bfloat16)
    dispatch = jnp.einsum(
        "tes,td->esd", dispatch_hot, moe_in, preferred_element_type=jnp.float32
    ).astype(jnp.bfloat16)
    combine = jnp.sum(
        pair_hot * routing_gate_weight[:, :, None, None], axis=1
    )
    arrived = lax.all_to_all(dispatch, "expert", split_axis=0, concat_axis=0, tiled=True)
    gate_out = jnp.einsum(
        "esd,fd->esf", arrived, gate_up_full[0], preferred_element_type=jnp.float32
    )
    up_out = jnp.einsum(
        "esd,fd->esf", arrived, gate_up_full[1], preferred_element_type=jnp.float32
    )
    activation = (jax.nn.silu(gate_out) * up_out).astype(jnp.bfloat16)
    block_units = expert_gate_up_weight.shape[1]
    block_count = down_full.shape[0] // block_units
    summed = jnp.zeros(arrived.shape, jnp.float32)
    for quarter in range(block_count):
        part = jnp.einsum(
            "esf,fd->esd",
            activation[:, :, quarter * block_units : (quarter + 1) * block_units],
            down_full[quarter * block_units : (quarter + 1) * block_units],
            preferred_element_type=jnp.float32,
        )
        summed = summed + part.astype(jnp.bfloat16).astype(jnp.float32)
    expert_rows = summed.astype(jnp.bfloat16)
    returned = lax.all_to_all(expert_rows, "expert", split_axis=0, concat_axis=0, tiled=True)
    moe = jnp.einsum(
        "tes,esd->td",
        combine,
        returned.astype(jnp.float32),
        precision=lax.Precision.HIGHEST,
        preferred_element_type=jnp.float32,
    )
    return (mid.astype(jnp.float32) + moe).astype(jnp.bfloat16)


def solution(mesh):
    placed = (
        P(("dp", "expert"), None),
        P(("dp", "expert"), None),
        P(("dp", "expert"), None),
        P(("dp", "expert"), None),
        P("dp", "expert"),
        P("dp", None),
        P(),
        P(),
        P("dp", None, None),
        P("dp", None, None),
        P("dp", None, None),
        P("dp", None, None),
        P("dp", None, None),
        P(),
        P(),
        P("expert", "dp", None, None),
        P("expert", "dp", None),
        P(("dp", "expert"), None),
        P(("dp", "expert"), None),
    )
    return jax.shard_map(
        shards, mesh=mesh, in_specs=placed, out_specs=P(("dp", "expert"), None), check_vma=False
    )
```

```python
import jax
import jax.numpy as jnp
from jax import lax
from jax.sharding import PartitionSpec as P

HD = 64
ADAPTER_RANK = 16
TOP = 4


EPSILON = 1e-05
ROPE_BASE = 150000.0
SCORE_SCALE = 0.125
NEGATIVE = -1e30


def rms_scale(rows_in, gain):
    floats = rows_in.astype(jnp.float32)
    mean_square = jnp.mean(floats * floats, axis=-1, keepdims=True)
    return (floats * lax.rsqrt(mean_square + EPSILON) * gain).astype(jnp.bfloat16)


def rotate(heads, positions):
    head_dim = heads.shape[-1]
    half = head_dim // 2
    freqs = ROPE_BASE ** (-(2.0 * jnp.arange(half, dtype=jnp.float32) / head_dim))
    angle = positions.astype(jnp.float32)[:, None] * freqs[None, :]
    cosine = jnp.cos(angle)[:, None, :]
    sine = jnp.sin(angle)[:, None, :]
    first = heads[..., :half]
    second = heads[..., half:]
    return jnp.concatenate(
        [first * cosine - second * sine, second * cosine + first * sine], axis=-1
    )


def multiply_rows(left, right):
    return lax.dot_general(
        left, right, (((1,), (1,)), ((), ())), preferred_element_type=jnp.float32
    )


def select_adapter(all_terms, adapter_selector, span):
    stacked = all_terms.reshape(all_terms.shape[0], adapter_selector.shape[1], span)
    return jnp.sum(stacked * adapter_selector[:, :, None], axis=1)


def spread(adapter_selector, low_part):
    joined = adapter_selector[:, :, None] * low_part.astype(jnp.float32)[:, None, :]
    return joined.reshape(joined.shape[0], -1).astype(jnp.bfloat16)


def expert_hidden(rows_in, gate_up):
    gate_out = multiply_rows(rows_in, gate_up[:, 0, :])
    up_out = multiply_rows(rows_in, gate_up[:, 1, :])
    return (jax.nn.silu(gate_out) * up_out).astype(jnp.bfloat16)


def gather_expert_blocks(gate_up_local, down_local, anchor=None):
    count = lax.axis_size("dp")
    if count != 4:
        gate_up_full = lax.all_gather(gate_up_local, "dp", axis=1, tiled=True)
        down_full = lax.all_gather(down_local, "dp", axis=0, tiled=True)
        return anchor, [(gate_up_full[0], gate_up_full[1], [down_full])]
    forward = [(i, (i + 1) % count) for i in range(count)]
    backward = [(i, (i - 1) % count) for i in range(count)]
    gate_up_prev, down_prev = lax.ppermute((gate_up_local, down_local), "dp", forward)
    gate_up_next, down_next = lax.ppermute((gate_up_local, down_local), "dp", backward)
    if anchor is not None:
        anchor, gate_up_prev, down_prev, gate_up_next, down_next = lax.optimization_barrier(
            (anchor, gate_up_prev, down_prev, gate_up_next, down_next)
        )
    half = down_local.shape[0] // 2
    far_gate, far_down_a = lax.ppermute((gate_up_prev[0], down_prev[:half]), "dp", forward)
    far_up, far_down_b = lax.ppermute((gate_up_next[1], down_next[half:]), "dp", backward)
    return anchor, [
        (gate_up_local[0], gate_up_local[1], [down_local]),
        (gate_up_prev[0], gate_up_prev[1], [down_prev]),
        (gate_up_next[0], gate_up_next[1], [down_next]),
        (far_gate, far_up, [far_down_a, far_down_b]),
    ]


def shards(
    hidden,
    query_base_rows,
    key_base_rows,
    value_base_rows,
    prompt_number,
    prompt_adapter,
    sinks,
    attention_gain,
    adapter_down_factors,
    query_up_factors,
    key_value_up_factors,
    output_down_factors,
    output_up_factors,
    attention_output_weight,
    expert_norm_gain,
    expert_gate_up_weight,
    expert_down_weight,
    routes,
    routing_gate_weight,
):
    tok_rows = hidden.shape[0]
    model_width = hidden.shape[1]
    q_width = query_base_rows.shape[1]
    kv_width = key_base_rows.shape[1]
    kv_heads = kv_width // HD
    groups = q_width // HD // kv_heads
    doc_count = prompt_adapter.shape[1]
    row_ids = lax.all_gather(prompt_number, "expert", axis=1, tiled=True)[0]
    my_ids = prompt_number[0]
    doc_range = jnp.arange(doc_count, dtype=jnp.int32)
    counts = jnp.sum((row_ids[:, None] == doc_range[None, :]).astype(jnp.int32), axis=0)
    firsts = jnp.cumsum(counts) - counts
    doc_hot = (my_ids[:, None] == doc_range[None, :]).astype(jnp.int32)
    query_index = lax.axis_index("expert") * tok_rows + jnp.arange(tok_rows, dtype=jnp.int32)
    positions = query_index - jnp.sum(doc_hot * firsts[None, :], axis=1)
    adapter_of = jnp.sum(doc_hot * prompt_adapter[0][None, :], axis=1)
    local_factors = (
        adapter_down_factors,
        query_up_factors,
        key_value_up_factors,
        output_down_factors,
        output_up_factors,
    )
    local_count = adapter_down_factors.shape[0]
    joined_factors = jnp.concatenate([f.reshape(local_count, -1) for f in local_factors], axis=1)
    all_factors = lax.all_gather(joined_factors, "dp", axis=0, tiled=True)
    factors = []
    offset = 0
    for f in local_factors:
        width = f.shape[1] * f.shape[2]
        factors.append(
            all_factors[:, offset : offset + width].reshape(all_factors.shape[0], f.shape[1], f.shape[2])
        )
        offset += width
    all_down, all_up_query, all_up_keyval, all_o_down, all_o_up = factors
    gate_up_local = jnp.transpose(expert_gate_up_weight[0], (1, 0, 2))
    gate_up_local, down_local, _ = lax.optimization_barrier(
        (gate_up_local, expert_down_weight[0], all_factors)
    )
    adapter_table = all_down.shape[0]
    adapter_selector = (
        adapter_of[:, None] == jnp.arange(adapter_table, dtype=jnp.int32)[None, :]
    ).astype(jnp.float32)
    normalized_tokens = rms_scale(hidden, attention_gain)
    lowrank_part = select_adapter(
        multiply_rows(
            normalized_tokens, all_down.reshape(adapter_table * 3 * ADAPTER_RANK, model_width)
        ),
        adapter_selector,
        3 * ADAPTER_RANK,
    ).astype(jnp.bfloat16)
    q_delta = jnp.dot(
        spread(adapter_selector, lowrank_part[:, :ADAPTER_RANK]),
        all_up_query.reshape(adapter_table * ADAPTER_RANK, q_width),
        preferred_element_type=jnp.float32,
    )
    k_delta = jnp.dot(
        spread(adapter_selector, lowrank_part[:, ADAPTER_RANK : 2 * ADAPTER_RANK]),
        all_up_keyval[:, :, :kv_width].reshape(adapter_table * ADAPTER_RANK, kv_width),
        preferred_element_type=jnp.float32,
    )
    v_delta = jnp.dot(
        spread(adapter_selector, lowrank_part[:, 2 * ADAPTER_RANK :]),
        all_up_keyval[:, :, kv_width:].reshape(adapter_table * ADAPTER_RANK, kv_width),
        preferred_element_type=jnp.float32,
    )
    queries = rotate(
        (query_base_rows.astype(jnp.float32) + q_delta).reshape(tok_rows, kv_heads * groups, HD),
        positions,
    )
    queries = queries.astype(jnp.bfloat16).reshape(tok_rows, kv_heads, groups, HD)
    key_rows = rotate(
        (key_base_rows.astype(jnp.float32) + k_delta).reshape(tok_rows, kv_heads, HD), positions
    )
    key_rows = key_rows.astype(jnp.bfloat16).reshape(tok_rows, kv_width)
    value_rows = (value_base_rows.astype(jnp.float32) + v_delta).astype(jnp.bfloat16)
    sink_grid = sinks.reshape(kv_heads, groups)
    running_max = jnp.broadcast_to(sink_grid[:, :, None], (kv_heads, groups, tok_rows))
    running_sum = jnp.ones((kv_heads, groups, tok_rows), jnp.float32)
    weighted = jnp.zeros((kv_heads, groups, tok_rows, HD), jnp.float32)
    piece_kv = lax.all_gather(
        jnp.concatenate([key_rows, value_rows], axis=1), "expert", axis=0, tiled=True
    )
    piece_rows = piece_kv.shape[0]
    piece_keys = piece_kv[:, :kv_width].reshape(piece_rows, kv_heads, HD)
    piece_values = piece_kv[:, kv_width:].reshape(piece_rows, kv_heads, HD)
    gate_up_local = jnp.transpose(expert_gate_up_weight[0], (1, 0, 2))
    window = min(piece_rows, piece_rows // 2 + tok_rows)
    window_start = jnp.clip(
        (lax.axis_index("expert") + 1) * tok_rows - window, 0, piece_rows - window
    )
    piece_keys = lax.dynamic_slice_in_dim(piece_keys, window_start, window, 0)
    piece_values = lax.dynamic_slice_in_dim(piece_values, window_start, window, 0)
    window_ids = lax.dynamic_slice_in_dim(row_ids, window_start, window, 0)
    key_index = window_start + jnp.arange(window, dtype=jnp.int32)
    scores = (
        jnp.einsum("tkgd,nkd->kgtn", queries, piece_keys, preferred_element_type=jnp.float32)
        * SCORE_SCALE
    )
    allowed = (key_index[None, :] <= query_index[:, None]) & (
        window_ids[None, :] == my_ids[:, None]
    )
    scores = jnp.where(allowed[None, None], scores, NEGATIVE)
    fresh_max = jnp.maximum(running_max, jnp.max(scores, axis=-1))
    exps = jnp.exp(scores - fresh_max[..., None])
    factor = jnp.exp(running_max - fresh_max)
    running_sum = running_sum * factor + jnp.sum(exps, axis=-1)
    weighted = weighted * factor[..., None] + jnp.einsum(
        "kgtn,nkd->kgtd",
        exps.astype(jnp.bfloat16),
        piece_values,
        preferred_element_type=jnp.float32,
    )
    attended = (
        jnp.transpose(weighted / running_sum[..., None], (2, 0, 1, 3))
        .reshape(tok_rows, q_width)
        .astype(jnp.bfloat16)
    )
    attended, expert_blocks = gather_expert_blocks(gate_up_local, down_local, attended)
    o_low = select_adapter(
        multiply_rows(attended, all_o_down.reshape(adapter_table * ADAPTER_RANK, q_width)),
        adapter_selector,
        ADAPTER_RANK,
    ).astype(jnp.bfloat16)
    projected = jnp.dot(attended, attention_output_weight, preferred_element_type=jnp.float32)
    projected = projected + jnp.dot(
        spread(adapter_selector, o_low),
        all_o_up.reshape(adapter_table * ADAPTER_RANK, model_width),
        preferred_element_type=jnp.float32,
    )
    mid = (hidden.astype(jnp.float32) + projected).astype(jnp.bfloat16)
    moe_in = rms_scale(mid, expert_norm_gain)
    exp_dev = expert_gate_up_weight.shape[0]
    experts = lax.axis_size("expert") * exp_dev
    capacity = 5 * tok_rows * TOP // (4 * experts)
    flat_routes = routes.reshape(tok_rows * TOP)
    route_hot = (flat_routes[:, None] == jnp.arange(experts, dtype=jnp.int32)[None, :]).astype(
        jnp.int32
    )
    before = jnp.cumsum(route_hot, axis=0) - route_hot
    slot_index = jnp.sum(before * route_hot, axis=1)
    slot_hot = (
        slot_index[:, None] == jnp.arange(capacity, dtype=jnp.int32)[None, :]
    ).astype(jnp.float32)
    pair_hot = route_hot.astype(jnp.float32)[:, :, None] * slot_hot[:, None, :]
    pair_hot = pair_hot.reshape(tok_rows, TOP, experts, capacity)
    dispatch_hot = jnp.sum(pair_hot, axis=1).astype(jnp.bfloat16)
    dispatch = jnp.einsum(
        "tes,td->esd", dispatch_hot, moe_in, preferred_element_type=jnp.float32
    ).astype(jnp.bfloat16)
    combine = jnp.sum(
        pair_hot * routing_gate_weight[:, :, None, None], axis=1
    )
    arrived = lax.all_to_all(dispatch, "expert", split_axis=0, concat_axis=0, tiled=True)
    summed = jnp.zeros(arrived.shape, jnp.float32)
    for gate_w, up_w, down_ws in expert_blocks:
        gate_out = jnp.einsum("esd,fd->esf", arrived, gate_w, preferred_element_type=jnp.float32)
        up_out = jnp.einsum("esd,fd->esf", arrived, up_w, preferred_element_type=jnp.float32)
        activation = (jax.nn.silu(gate_out) * up_out).astype(jnp.bfloat16)
        part = jnp.zeros(arrived.shape, jnp.float32)
        offset = 0
        for down_w in down_ws:
            part = part + jnp.einsum(
                "esf,fd->esd",
                activation[:, :, offset : offset + down_w.shape[0]],
                down_w,
                preferred_element_type=jnp.float32,
            )
            offset += down_w.shape[0]
        summed = summed + part.astype(jnp.bfloat16).astype(jnp.float32)
    expert_rows = summed.astype(jnp.bfloat16)
    returned = lax.all_to_all(expert_rows, "expert", split_axis=0, concat_axis=0, tiled=True)
    moe = jnp.einsum(
        "tes,esd->td",
        combine,
        returned.astype(jnp.float32),
        precision=lax.Precision.HIGHEST,
        preferred_element_type=jnp.float32,
    )
    return (mid.astype(jnp.float32) + moe).astype(jnp.bfloat16)


def solution(mesh):
    placed = (
        P(("dp", "expert"), None),
        P(("dp", "expert"), None),
        P(("dp", "expert"), None),
        P(("dp", "expert"), None),
        P("dp", "expert"),
        P("dp", None),
        P(),
        P(),
        P("dp", None, None),
        P("dp", None, None),
        P("dp", None, None),
        P("dp", None, None),
        P("dp", None, None),
        P(),
        P(),
        P("expert", "dp", None, None),
        P("expert", "dp", None),
        P(("dp", "expert"), None),
        P(("dp", "expert"), None),
    )
    return jax.shard_map(
        shards, mesh=mesh, in_specs=placed, out_specs=P(("dp", "expert"), None), check_vma=False
    )
```

```python
import jax
import jax.numpy as jnp
from jax import lax
from jax.sharding import PartitionSpec as P

HD = 64
ADAPTER_RANK = 16
TOP = 4


EPSILON = 1e-05
ROPE_BASE = 150000.0
SCORE_SCALE = 0.125
NEGATIVE = -1e30


def rms_scale(rows_in, gain):
    floats = rows_in.astype(jnp.float32)
    mean_square = jnp.mean(floats * floats, axis=-1, keepdims=True)
    return (floats * lax.rsqrt(mean_square + EPSILON) * gain).astype(jnp.bfloat16)


def rotate(heads, positions):
    head_dim = heads.shape[-1]
    half = head_dim // 2
    freqs = ROPE_BASE ** (-(2.0 * jnp.arange(half, dtype=jnp.float32) / head_dim))
    angle = positions.astype(jnp.float32)[:, None] * freqs[None, :]
    cosine = jnp.cos(angle)[:, None, :]
    sine = jnp.sin(angle)[:, None, :]
    first = heads[..., :half]
    second = heads[..., half:]
    return jnp.concatenate(
        [first * cosine - second * sine, second * cosine + first * sine], axis=-1
    )


def multiply_rows(left, right):
    return lax.dot_general(
        left, right, (((1,), (1,)), ((), ())), preferred_element_type=jnp.float32
    )


def select_adapter(all_terms, adapter_selector, span):
    stacked = all_terms.reshape(all_terms.shape[0], adapter_selector.shape[1], span)
    return jnp.sum(stacked * adapter_selector[:, :, None], axis=1)


def spread(adapter_selector, low_part):
    joined = adapter_selector[:, :, None] * low_part.astype(jnp.float32)[:, None, :]
    return joined.reshape(joined.shape[0], -1).astype(jnp.bfloat16)


def gather_expert_blocks(gate_up_local, down_local, anchor=None):
    count = lax.axis_size("dp")
    if count != 4:
        gate_up_full = lax.all_gather(gate_up_local, "dp", axis=1, tiled=True)
        down_full = lax.all_gather(down_local, "dp", axis=0, tiled=True)
        return anchor, [(gate_up_full[0], gate_up_full[1], [down_full])]
    forward = [(i, (i + 1) % count) for i in range(count)]
    backward = [(i, (i - 1) % count) for i in range(count)]
    gate_up_prev, down_prev = lax.ppermute((gate_up_local, down_local), "dp", forward)
    gate_up_next, down_next = lax.ppermute((gate_up_local, down_local), "dp", backward)
    if anchor is not None:
        anchor, gate_up_prev, down_prev, gate_up_next, down_next = lax.optimization_barrier(
            (anchor, gate_up_prev, down_prev, gate_up_next, down_next)
        )
    half = down_local.shape[0] // 2
    far_gate, far_down_a = lax.ppermute((gate_up_prev[0], down_prev[:half]), "dp", forward)
    far_up, far_down_b = lax.ppermute((gate_up_next[1], down_next[half:]), "dp", backward)
    return anchor, [
        (gate_up_local[0], gate_up_local[1], [down_local]),
        (gate_up_prev[0], gate_up_prev[1], [down_prev]),
        (gate_up_next[0], gate_up_next[1], [down_next]),
        (far_gate, far_up, [far_down_a, far_down_b]),
    ]


def shards(
    hidden,
    query_base_rows,
    key_base_rows,
    value_base_rows,
    prompt_number,
    prompt_adapter,
    sinks,
    attention_gain,
    adapter_down_factors,
    query_up_factors,
    key_value_up_factors,
    output_down_factors,
    output_up_factors,
    attention_output_weight,
    expert_norm_gain,
    expert_gate_up_weight,
    expert_down_weight,
    routes,
    routing_gate_weight,
):
    tok_rows = hidden.shape[0]
    model_width = hidden.shape[1]
    q_width = query_base_rows.shape[1]
    kv_width = key_base_rows.shape[1]
    kv_heads = kv_width // HD
    groups = q_width // HD // kv_heads
    doc_count = prompt_adapter.shape[1]
    row_ids = lax.all_gather(prompt_number, "expert", axis=1, tiled=True)[0]
    my_ids = prompt_number[0]
    doc_range = jnp.arange(doc_count, dtype=jnp.int32)
    counts = jnp.sum((row_ids[:, None] == doc_range[None, :]).astype(jnp.int32), axis=0)
    firsts = jnp.cumsum(counts) - counts
    doc_hot = (my_ids[:, None] == doc_range[None, :]).astype(jnp.int32)
    query_index = lax.axis_index("expert") * tok_rows + jnp.arange(tok_rows, dtype=jnp.int32)
    positions = query_index - jnp.sum(doc_hot * firsts[None, :], axis=1)
    adapter_of = jnp.sum(doc_hot * prompt_adapter[0][None, :], axis=1)
    local_factors = (
        adapter_down_factors,
        query_up_factors,
        key_value_up_factors,
        output_down_factors,
        output_up_factors,
    )
    local_count = adapter_down_factors.shape[0]
    joined_factors = jnp.concatenate([f.reshape(local_count, -1) for f in local_factors], axis=1)
    all_factors = lax.all_gather(joined_factors, "dp", axis=0, tiled=True)
    factors = []
    offset = 0
    for f in local_factors:
        width = f.shape[1] * f.shape[2]
        factors.append(
            all_factors[:, offset : offset + width].reshape(all_factors.shape[0], f.shape[1], f.shape[2])
        )
        offset += width
    all_down, all_up_query, all_up_keyval, all_o_down, all_o_up = factors
    gate_up_local = jnp.transpose(expert_gate_up_weight[0], (1, 0, 2))
    down_local = expert_down_weight[0]
    adapter_table = all_down.shape[0]
    adapter_selector = (
        adapter_of[:, None] == jnp.arange(adapter_table, dtype=jnp.int32)[None, :]
    ).astype(jnp.float32)
    normalized_tokens = rms_scale(hidden, attention_gain)
    lowrank_part = select_adapter(
        multiply_rows(
            normalized_tokens, all_down.reshape(adapter_table * 3 * ADAPTER_RANK, model_width)
        ),
        adapter_selector,
        3 * ADAPTER_RANK,
    ).astype(jnp.bfloat16)
    q_delta = jnp.dot(
        spread(adapter_selector, lowrank_part[:, :ADAPTER_RANK]),
        all_up_query.reshape(adapter_table * ADAPTER_RANK, q_width),
        preferred_element_type=jnp.float32,
    )
    k_delta = jnp.dot(
        spread(adapter_selector, lowrank_part[:, ADAPTER_RANK : 2 * ADAPTER_RANK]),
        all_up_keyval[:, :, :kv_width].reshape(adapter_table * ADAPTER_RANK, kv_width),
        preferred_element_type=jnp.float32,
    )
    v_delta = jnp.dot(
        spread(adapter_selector, lowrank_part[:, 2 * ADAPTER_RANK :]),
        all_up_keyval[:, :, kv_width:].reshape(adapter_table * ADAPTER_RANK, kv_width),
        preferred_element_type=jnp.float32,
    )
    queries = rotate(
        (query_base_rows.astype(jnp.float32) + q_delta).reshape(tok_rows, kv_heads * groups, HD),
        positions,
    )
    queries = queries.astype(jnp.bfloat16).reshape(tok_rows, kv_heads, groups, HD)
    key_rows = rotate(
        (key_base_rows.astype(jnp.float32) + k_delta).reshape(tok_rows, kv_heads, HD), positions
    )
    key_rows = key_rows.astype(jnp.bfloat16).reshape(tok_rows, kv_width)
    value_rows = (value_base_rows.astype(jnp.float32) + v_delta).astype(jnp.bfloat16)
    sink_grid = sinks.reshape(kv_heads, groups)
    running_max = jnp.broadcast_to(sink_grid[:, :, None], (kv_heads, groups, tok_rows))
    running_sum = jnp.ones((kv_heads, groups, tok_rows), jnp.float32)
    weighted = jnp.zeros((kv_heads, groups, tok_rows, HD), jnp.float32)
    piece_kv = lax.all_gather(
        jnp.concatenate([key_rows, value_rows], axis=1), "expert", axis=0, tiled=True
    )
    piece_rows = piece_kv.shape[0]
    piece_keys = piece_kv[:, :kv_width].reshape(piece_rows, kv_heads, HD)
    piece_values = piece_kv[:, kv_width:].reshape(piece_rows, kv_heads, HD)
    gate_up_local = jnp.transpose(expert_gate_up_weight[0], (1, 0, 2))
    window = min(piece_rows, piece_rows // 2 + tok_rows)
    window_start = jnp.clip(
        (lax.axis_index("expert") + 1) * tok_rows - window, 0, piece_rows - window
    )
    piece_keys = lax.dynamic_slice_in_dim(piece_keys, window_start, window, 0)
    piece_values = lax.dynamic_slice_in_dim(piece_values, window_start, window, 0)
    window_ids = lax.dynamic_slice_in_dim(row_ids, window_start, window, 0)
    key_index = window_start + jnp.arange(window, dtype=jnp.int32)
    scores = (
        jnp.einsum("tkgd,nkd->kgtn", queries, piece_keys, preferred_element_type=jnp.float32)
        * SCORE_SCALE
    )
    allowed = (key_index[None, :] <= query_index[:, None]) & (
        window_ids[None, :] == my_ids[:, None]
    )
    scores = jnp.where(allowed[None, None], scores, NEGATIVE)
    fresh_max = jnp.maximum(running_max, jnp.max(scores, axis=-1))
    exps = jnp.exp(scores - fresh_max[..., None])
    factor = jnp.exp(running_max - fresh_max)
    running_sum = running_sum * factor + jnp.sum(exps, axis=-1)
    weighted = weighted * factor[..., None] + jnp.einsum(
        "kgtn,nkd->kgtd",
        exps.astype(jnp.bfloat16),
        piece_values,
        preferred_element_type=jnp.float32,
    )
    attended = (
        jnp.transpose(weighted / running_sum[..., None], (2, 0, 1, 3))
        .reshape(tok_rows, q_width)
        .astype(jnp.bfloat16)
    )
    _, expert_blocks = gather_expert_blocks(gate_up_local, down_local)
    o_low = select_adapter(
        multiply_rows(attended, all_o_down.reshape(adapter_table * ADAPTER_RANK, q_width)),
        adapter_selector,
        ADAPTER_RANK,
    ).astype(jnp.bfloat16)
    projected = jnp.dot(attended, attention_output_weight, preferred_element_type=jnp.float32)
    projected = projected + jnp.dot(
        spread(adapter_selector, o_low),
        all_o_up.reshape(adapter_table * ADAPTER_RANK, model_width),
        preferred_element_type=jnp.float32,
    )
    mid = (hidden.astype(jnp.float32) + projected).astype(jnp.bfloat16)
    moe_in = rms_scale(mid, expert_norm_gain)
    exp_dev = expert_gate_up_weight.shape[0]
    experts = lax.axis_size("expert") * exp_dev
    capacity = 5 * tok_rows * TOP // (4 * experts)
    flat_routes = routes.reshape(tok_rows * TOP)
    route_hot = (flat_routes[:, None] == jnp.arange(experts, dtype=jnp.int32)[None, :]).astype(
        jnp.int32
    )
    before = jnp.cumsum(route_hot, axis=0) - route_hot
    slot_index = jnp.sum(before * route_hot, axis=1)
    slot_hot = (
        slot_index[:, None] == jnp.arange(capacity, dtype=jnp.int32)[None, :]
    ).astype(jnp.float32)
    pair_hot = route_hot.astype(jnp.float32)[:, :, None] * slot_hot[:, None, :]
    pair_hot = pair_hot.reshape(tok_rows, TOP, experts, capacity)
    dispatch_hot = jnp.sum(pair_hot, axis=1).astype(jnp.bfloat16)
    dispatch = jnp.einsum(
        "tes,td->esd", dispatch_hot, moe_in, preferred_element_type=jnp.float32
    ).astype(jnp.bfloat16)
    combine = jnp.sum(
        pair_hot * routing_gate_weight[:, :, None, None], axis=1
    )
    arrived = lax.all_to_all(dispatch, "expert", split_axis=0, concat_axis=0, tiled=True)
    summed = jnp.zeros(arrived.shape, jnp.float32)
    for gate_w, up_w, down_ws in expert_blocks:
        gate_out = jnp.einsum("esd,fd->esf", arrived, gate_w, preferred_element_type=jnp.float32)
        up_out = jnp.einsum("esd,fd->esf", arrived, up_w, preferred_element_type=jnp.float32)
        activation = (jax.nn.silu(gate_out) * up_out).astype(jnp.bfloat16)
        part = jnp.zeros(arrived.shape, jnp.float32)
        offset = 0
        for down_w in down_ws:
            part = part + jnp.einsum(
                "esf,fd->esd",
                activation[:, :, offset : offset + down_w.shape[0]],
                down_w,
                preferred_element_type=jnp.float32,
            )
            offset += down_w.shape[0]
        summed = summed + part.astype(jnp.bfloat16).astype(jnp.float32)
    expert_rows = summed.astype(jnp.bfloat16)
    returned = lax.all_to_all(expert_rows, "expert", split_axis=0, concat_axis=0, tiled=True)
    moe = jnp.einsum(
        "tes,esd->td",
        combine,
        returned.astype(jnp.float32),
        precision=lax.Precision.HIGHEST,
        preferred_element_type=jnp.float32,
    )
    return (mid.astype(jnp.float32) + moe).astype(jnp.bfloat16)


def solution(mesh):
    placed = (
        P(("dp", "expert"), None),
        P(("dp", "expert"), None),
        P(("dp", "expert"), None),
        P(("dp", "expert"), None),
        P("dp", "expert"),
        P("dp", None),
        P(),
        P(),
        P("dp", None, None),
        P("dp", None, None),
        P("dp", None, None),
        P("dp", None, None),
        P("dp", None, None),
        P(),
        P(),
        P("expert", "dp", None, None),
        P("expert", "dp", None),
        P(("dp", "expert"), None),
        P(("dp", "expert"), None),
    )

    return jax.shard_map(
        shards, mesh=mesh, in_specs=placed, out_specs=P(("dp", "expert"), None), check_vma=False
    )
```

```python
import jax
import jax.numpy as jnp
from jax import lax
from jax.sharding import PartitionSpec as P

HD = 64
ADAPTER_RANK = 16
TOP = 4


EPSILON = 1e-05
ROPE_BASE = 150000.0
SCORE_SCALE = 0.125
NEGATIVE = -1e30


def rms_scale(rows_in, gain):
    floats = rows_in.astype(jnp.float32)
    mean_square = jnp.mean(floats * floats, axis=-1, keepdims=True)
    return (floats * lax.rsqrt(mean_square + EPSILON) * gain).astype(jnp.bfloat16)


def rotate(heads, positions):
    head_dim = heads.shape[-1]
    half = head_dim // 2
    freqs = ROPE_BASE ** (-(2.0 * jnp.arange(half, dtype=jnp.float32) / head_dim))
    angle = positions.astype(jnp.float32)[:, None] * freqs[None, :]
    cosine = jnp.cos(angle)[:, None, :]
    sine = jnp.sin(angle)[:, None, :]
    first = heads[..., :half]
    second = heads[..., half:]
    return jnp.concatenate(
        [first * cosine - second * sine, second * cosine + first * sine], axis=-1
    )


def multiply_rows(left, right):
    return lax.dot_general(
        left, right, (((1,), (1,)), ((), ())), preferred_element_type=jnp.float32
    )


def select_adapter(all_terms, adapter_selector, span):
    stacked = all_terms.reshape(all_terms.shape[0], adapter_selector.shape[1], span)
    return jnp.sum(stacked * adapter_selector[:, :, None], axis=1)


def spread(adapter_selector, low_part):
    joined = adapter_selector[:, :, None] * low_part.astype(jnp.float32)[:, None, :]
    return joined.reshape(joined.shape[0], -1).astype(jnp.bfloat16)


def gather_expert_blocks(gate_up_local, down_local, anchor=None):
    count = lax.axis_size("dp")
    if count != 4:
        gate_up_full = lax.all_gather(gate_up_local, "dp", axis=1, tiled=True)
        down_full = lax.all_gather(down_local, "dp", axis=0, tiled=True)
        return anchor, [(gate_up_full[0], gate_up_full[1], [down_full])]
    forward = [(i, (i + 1) % count) for i in range(count)]
    backward = [(i, (i - 1) % count) for i in range(count)]
    gate_up_prev, down_prev = lax.ppermute((gate_up_local, down_local), "dp", forward)
    gate_up_next, down_next = lax.ppermute((gate_up_local, down_local), "dp", backward)
    if anchor is not None:
        anchor, gate_up_prev, down_prev, gate_up_next, down_next = lax.optimization_barrier(
            (anchor, gate_up_prev, down_prev, gate_up_next, down_next)
        )
    half = down_local.shape[0] // 2
    far_gate, far_down_a = lax.ppermute((gate_up_prev[0], down_prev[:half]), "dp", forward)
    far_up, far_down_b = lax.ppermute((gate_up_next[1], down_next[half:]), "dp", backward)
    return anchor, [
        (gate_up_local[0], gate_up_local[1], [down_local]),
        (gate_up_prev[0], gate_up_prev[1], [down_prev]),
        (gate_up_next[0], gate_up_next[1], [down_next]),
        (far_gate, far_up, [far_down_a, far_down_b]),
    ]


def shards(
    hidden,
    query_base_rows,
    key_base_rows,
    value_base_rows,
    prompt_number,
    prompt_adapter,
    sinks,
    attention_gain,
    adapter_down_factors,
    query_up_factors,
    key_value_up_factors,
    output_down_factors,
    output_up_factors,
    attention_output_weight,
    expert_norm_gain,
    expert_gate_up_weight,
    expert_down_weight,
    routes,
    routing_gate_weight,
):
    tok_rows = hidden.shape[0]
    model_width = hidden.shape[1]
    q_width = query_base_rows.shape[1]
    kv_width = key_base_rows.shape[1]
    kv_heads = kv_width // HD
    groups = q_width // HD // kv_heads
    doc_count = prompt_adapter.shape[1]
    row_ids = lax.all_gather(prompt_number, "expert", axis=1, tiled=True)[0]
    my_ids = prompt_number[0]
    doc_range = jnp.arange(doc_count, dtype=jnp.int32)
    counts = jnp.sum((row_ids[:, None] == doc_range[None, :]).astype(jnp.int32), axis=0)
    firsts = jnp.cumsum(counts) - counts
    doc_hot = (my_ids[:, None] == doc_range[None, :]).astype(jnp.int32)
    query_index = lax.axis_index("expert") * tok_rows + jnp.arange(tok_rows, dtype=jnp.int32)
    positions = query_index - jnp.sum(doc_hot * firsts[None, :], axis=1)
    adapter_of = jnp.sum(doc_hot * prompt_adapter[0][None, :], axis=1)
    local_factors = (
        adapter_down_factors,
        query_up_factors,
        key_value_up_factors,
        output_down_factors,
        output_up_factors,
    )
    local_count = adapter_down_factors.shape[0]
    joined_factors = jnp.concatenate([f.reshape(local_count, -1) for f in local_factors], axis=1)
    all_factors = lax.all_gather(joined_factors, "dp", axis=0, tiled=False)
    adapter_total = all_factors.shape[0] * local_count
    factors = []
    offset = 0
    for f in local_factors:
        width = f.shape[1] * f.shape[2]
        factors.append(
            all_factors[:, :, offset : offset + width].reshape(adapter_total, f.shape[1], f.shape[2])
        )
        offset += width
    all_down, all_up_query, all_up_keyval, all_o_down, all_o_up = factors
    gate_up_local = jnp.transpose(expert_gate_up_weight[0], (1, 0, 2))
    down_local = expert_down_weight[0]
    adapter_table = all_down.shape[0]
    adapter_selector = (
        adapter_of[:, None] == jnp.arange(adapter_table, dtype=jnp.int32)[None, :]
    ).astype(jnp.float32)
    normalized_tokens = rms_scale(hidden, attention_gain)
    lowrank_part = select_adapter(
        multiply_rows(
            normalized_tokens, all_down.reshape(adapter_table * 3 * ADAPTER_RANK, model_width)
        ),
        adapter_selector,
        3 * ADAPTER_RANK,
    ).astype(jnp.bfloat16)
    q_delta = jnp.dot(
        spread(adapter_selector, lowrank_part[:, :ADAPTER_RANK]),
        all_up_query.reshape(adapter_table * ADAPTER_RANK, q_width),
        preferred_element_type=jnp.float32,
    )
    k_delta = jnp.dot(
        spread(adapter_selector, lowrank_part[:, ADAPTER_RANK : 2 * ADAPTER_RANK]),
        all_up_keyval[:, :, :kv_width].reshape(adapter_table * ADAPTER_RANK, kv_width),
        preferred_element_type=jnp.float32,
    )
    v_delta = jnp.dot(
        spread(adapter_selector, lowrank_part[:, 2 * ADAPTER_RANK :]),
        all_up_keyval[:, :, kv_width:].reshape(adapter_table * ADAPTER_RANK, kv_width),
        preferred_element_type=jnp.float32,
    )
    queries = rotate(
        (query_base_rows.astype(jnp.float32) + q_delta).reshape(tok_rows, kv_heads * groups, HD),
        positions,
    )
    queries = queries.astype(jnp.bfloat16).reshape(tok_rows, kv_heads, groups, HD)
    key_rows = rotate(
        (key_base_rows.astype(jnp.float32) + k_delta).reshape(tok_rows, kv_heads, HD), positions
    )
    key_rows = key_rows.astype(jnp.bfloat16).reshape(tok_rows, kv_width)
    value_rows = (value_base_rows.astype(jnp.float32) + v_delta).astype(jnp.bfloat16)
    sink_grid = sinks.reshape(kv_heads, groups)
    running_max = jnp.broadcast_to(sink_grid[:, :, None], (kv_heads, groups, tok_rows))
    running_sum = jnp.ones((kv_heads, groups, tok_rows), jnp.float32)
    weighted = jnp.zeros((kv_heads, groups, tok_rows, HD), jnp.float32)
    piece_kv = lax.all_gather(
        jnp.concatenate([key_rows, value_rows], axis=1), "expert", axis=0, tiled=True
    )
    piece_rows = piece_kv.shape[0]
    piece_keys = piece_kv[:, :kv_width].reshape(piece_rows, kv_heads, HD)
    piece_values = piece_kv[:, kv_width:].reshape(piece_rows, kv_heads, HD)
    gate_up_local = jnp.transpose(expert_gate_up_weight[0], (1, 0, 2))
    window = min(piece_rows, piece_rows // 2 + tok_rows)
    window_start = jnp.clip(
        (lax.axis_index("expert") + 1) * tok_rows - window, 0, piece_rows - window
    )
    piece_keys = lax.dynamic_slice_in_dim(piece_keys, window_start, window, 0)
    piece_values = lax.dynamic_slice_in_dim(piece_values, window_start, window, 0)
    window_ids = lax.dynamic_slice_in_dim(row_ids, window_start, window, 0)
    key_index = window_start + jnp.arange(window, dtype=jnp.int32)
    scores = (
        jnp.einsum("tkgd,nkd->kgtn", queries, piece_keys, preferred_element_type=jnp.float32)
        * SCORE_SCALE
    )
    allowed = (key_index[None, :] <= query_index[:, None]) & (
        window_ids[None, :] == my_ids[:, None]
    )
    scores = jnp.where(allowed[None, None], scores, NEGATIVE)
    fresh_max = jnp.maximum(running_max, jnp.max(scores, axis=-1))
    exps = jnp.exp(scores - fresh_max[..., None])
    factor = jnp.exp(running_max - fresh_max)
    running_sum = running_sum * factor + jnp.sum(exps, axis=-1)
    weighted = weighted * factor[..., None] + jnp.einsum(
        "kgtn,nkd->kgtd",
        exps.astype(jnp.bfloat16),
        piece_values,
        preferred_element_type=jnp.float32,
    )
    attended = (
        jnp.transpose(weighted / running_sum[..., None], (2, 0, 1, 3))
        .reshape(tok_rows, q_width)
        .astype(jnp.bfloat16)
    )
    _, expert_blocks = gather_expert_blocks(gate_up_local, down_local)
    o_low = select_adapter(
        multiply_rows(attended, all_o_down.reshape(adapter_table * ADAPTER_RANK, q_width)),
        adapter_selector,
        ADAPTER_RANK,
    ).astype(jnp.bfloat16)
    projected = jnp.dot(attended, attention_output_weight, preferred_element_type=jnp.float32)
    projected = projected + jnp.dot(
        spread(adapter_selector, o_low),
        all_o_up.reshape(adapter_table * ADAPTER_RANK, model_width),
        preferred_element_type=jnp.float32,
    )
    mid = (hidden.astype(jnp.float32) + projected).astype(jnp.bfloat16)
    moe_in = rms_scale(mid, expert_norm_gain)
    exp_dev = expert_gate_up_weight.shape[0]
    experts = lax.axis_size("expert") * exp_dev
    capacity = 5 * tok_rows * TOP // (4 * experts)
    flat_routes = routes.reshape(tok_rows * TOP)
    route_hot = (flat_routes[:, None] == jnp.arange(experts, dtype=jnp.int32)[None, :]).astype(
        jnp.int32
    )
    before = jnp.cumsum(route_hot, axis=0) - route_hot
    slot_index = jnp.sum(before * route_hot, axis=1)
    slot_hot = (
        slot_index[:, None] == jnp.arange(capacity, dtype=jnp.int32)[None, :]
    ).astype(jnp.float32)
    pair_hot = route_hot.astype(jnp.float32)[:, :, None] * slot_hot[:, None, :]
    pair_hot = pair_hot.reshape(tok_rows, TOP, experts, capacity)
    dispatch_hot = jnp.sum(pair_hot, axis=1).astype(jnp.bfloat16)
    dispatch = jnp.einsum(
        "tes,td->esd", dispatch_hot, moe_in, preferred_element_type=jnp.float32
    ).astype(jnp.bfloat16)
    combine = jnp.sum(
        pair_hot * routing_gate_weight[:, :, None, None], axis=1
    )
    arrived = lax.all_to_all(dispatch, "expert", split_axis=0, concat_axis=0, tiled=True)
    summed = jnp.zeros(arrived.shape, jnp.float32)
    for gate_w, up_w, down_ws in expert_blocks:
        gate_out = jnp.einsum("esd,fd->esf", arrived, gate_w, preferred_element_type=jnp.float32)
        up_out = jnp.einsum("esd,fd->esf", arrived, up_w, preferred_element_type=jnp.float32)
        activation = (jax.nn.silu(gate_out) * up_out).astype(jnp.bfloat16)
        part = jnp.zeros(arrived.shape, jnp.float32)
        offset = 0
        for down_w in down_ws:
            part = part + jnp.einsum(
                "esf,fd->esd",
                activation[:, :, offset : offset + down_w.shape[0]],
                down_w,
                preferred_element_type=jnp.float32,
            )
            offset += down_w.shape[0]
        summed = summed + part.astype(jnp.bfloat16).astype(jnp.float32)
    expert_rows = summed.astype(jnp.bfloat16)
    returned = lax.all_to_all(expert_rows, "expert", split_axis=0, concat_axis=0, tiled=True)
    moe = jnp.einsum(
        "tes,esd->td",
        combine,
        returned.astype(jnp.float32),
        precision=lax.Precision.HIGHEST,
        preferred_element_type=jnp.float32,
    )
    return (mid.astype(jnp.float32) + moe).astype(jnp.bfloat16)


def solution(mesh):
    placed = (
        P(("dp", "expert"), None),
        P(("dp", "expert"), None),
        P(("dp", "expert"), None),
        P(("dp", "expert"), None),
        P("dp", "expert"),
        P("dp", None),
        P(),
        P(),
        P("dp", None, None),
        P("dp", None, None),
        P("dp", None, None),
        P("dp", None, None),
        P("dp", None, None),
        P(),
        P(),
        P("expert", "dp", None, None),
        P("expert", "dp", None),
        P(("dp", "expert"), None),
        P(("dp", "expert"), None),
    )

    return jax.shard_map(
        shards, mesh=mesh, in_specs=placed, out_specs=P(("dp", "expert"), None), check_vma=False
    )
```

```python
import jax
import jax.numpy as jnp
from jax import lax
from jax.sharding import PartitionSpec as P

HD = 64
ADAPTER_RANK = 16
TOP = 4


EPSILON = 1e-05
ROPE_BASE = 150000.0
SCORE_SCALE = 0.125
NEGATIVE = -1e30


def rms_scale(rows_in, gain):
    floats = rows_in.astype(jnp.float32)
    mean_square = jnp.mean(floats * floats, axis=-1, keepdims=True)
    return (floats * lax.rsqrt(mean_square + EPSILON) * gain).astype(jnp.bfloat16)


def rotate(heads, positions):
    head_dim = heads.shape[-1]
    half = head_dim // 2
    freqs = ROPE_BASE ** (-(2.0 * jnp.arange(half, dtype=jnp.float32) / head_dim))
    angle = positions.astype(jnp.float32)[:, None] * freqs[None, :]
    cosine = jnp.cos(angle)[:, None, :]
    sine = jnp.sin(angle)[:, None, :]
    first = heads[..., :half]
    second = heads[..., half:]
    return jnp.concatenate(
        [first * cosine - second * sine, second * cosine + first * sine], axis=-1
    )


def multiply_rows(left, right):
    return lax.dot_general(
        left, right, (((1,), (1,)), ((), ())), preferred_element_type=jnp.float32
    )


def select_adapter(all_terms, adapter_selector, span):
    stacked = all_terms.reshape(all_terms.shape[0], adapter_selector.shape[1], span)
    return jnp.sum(stacked * adapter_selector[:, :, None], axis=1)


def spread(adapter_selector, low_part):
    joined = adapter_selector[:, :, None] * low_part.astype(jnp.float32)[:, None, :]
    return joined.reshape(joined.shape[0], -1).astype(jnp.bfloat16)


def gather_expert_blocks(gate_up_local, down_local, anchor=None):
    count = lax.axis_size("dp")
    if count != 4:
        gate_up_full = lax.all_gather(gate_up_local, "dp", axis=1, tiled=True)
        down_full = lax.all_gather(down_local, "dp", axis=0, tiled=True)
        return anchor, [(gate_up_full[0], gate_up_full[1], [down_full])]
    forward = [(i, (i + 1) % count) for i in range(count)]
    backward = [(i, (i - 1) % count) for i in range(count)]
    gate_up_prev, down_prev = lax.ppermute((gate_up_local, down_local), "dp", forward)
    gate_up_next, down_next = lax.ppermute((gate_up_local, down_local), "dp", backward)
    if anchor is not None:
        anchor, gate_up_prev, down_prev, gate_up_next, down_next = lax.optimization_barrier(
            (anchor, gate_up_prev, down_prev, gate_up_next, down_next)
        )
    half = down_local.shape[0] // 2
    far_gate, far_down_a = lax.ppermute((gate_up_prev[0], down_prev[:half]), "dp", forward)
    far_up, far_down_b = lax.ppermute((gate_up_next[1], down_next[half:]), "dp", backward)
    return anchor, [
        (gate_up_local[0], gate_up_local[1], [down_local]),
        (gate_up_prev[0], gate_up_prev[1], [down_prev]),
        (gate_up_next[0], gate_up_next[1], [down_next]),
        (far_gate, far_up, [far_down_a, far_down_b]),
    ]


def shards(
    hidden,
    query_base_rows,
    key_base_rows,
    value_base_rows,
    prompt_number,
    prompt_adapter,
    sinks,
    attention_gain,
    adapter_down_factors,
    query_up_factors,
    key_value_up_factors,
    output_down_factors,
    output_up_factors,
    attention_output_weight,
    expert_norm_gain,
    expert_gate_up_weight,
    expert_down_weight,
    routes,
    routing_gate_weight,
):
    tok_rows = hidden.shape[0]
    model_width = hidden.shape[1]
    q_width = query_base_rows.shape[1]
    kv_width = key_base_rows.shape[1]
    kv_heads = kv_width // HD
    groups = q_width // HD // kv_heads
    doc_count = prompt_adapter.shape[1]
    row_ids = lax.all_gather(prompt_number, "expert", axis=1, tiled=True)[0]
    my_ids = prompt_number[0]
    doc_range = jnp.arange(doc_count, dtype=jnp.int32)
    counts = jnp.sum((row_ids[:, None] == doc_range[None, :]).astype(jnp.int32), axis=0)
    firsts = jnp.cumsum(counts) - counts
    doc_hot = (my_ids[:, None] == doc_range[None, :]).astype(jnp.int32)
    query_index = lax.axis_index("expert") * tok_rows + jnp.arange(tok_rows, dtype=jnp.int32)
    positions = query_index - jnp.sum(doc_hot * firsts[None, :], axis=1)
    adapter_of = jnp.sum(doc_hot * prompt_adapter[0][None, :], axis=1)
    local_factors = (
        adapter_down_factors,
        query_up_factors,
        key_value_up_factors,
        output_down_factors,
        output_up_factors,
    )
    local_count = adapter_down_factors.shape[0]
    rest_factors = local_factors[1:]
    joined_factors = jnp.concatenate([f.reshape(local_count, -1) for f in rest_factors], axis=1)
    all_down = lax.all_gather(adapter_down_factors, "dp", axis=0, tiled=True)
    rest_gathered = lax.all_gather(joined_factors, "dp", axis=0, tiled=False)
    adapter_total = rest_gathered.shape[0] * local_count
    factors = [all_down]
    offset = 0
    for f in rest_factors:
        width = f.shape[1] * f.shape[2]
        factors.append(
            rest_gathered[:, :, offset : offset + width].reshape(adapter_total, f.shape[1], f.shape[2])
        )
        offset += width
    all_down, all_up_query, all_up_keyval, all_o_down, all_o_up = factors
    gate_up_local = jnp.transpose(expert_gate_up_weight[0], (1, 0, 2))
    down_local = expert_down_weight[0]
    adapter_table = all_down.shape[0]
    adapter_selector = (
        adapter_of[:, None] == jnp.arange(adapter_table, dtype=jnp.int32)[None, :]
    ).astype(jnp.float32)
    normalized_tokens = rms_scale(hidden, attention_gain)
    lowrank_part = select_adapter(
        multiply_rows(
            normalized_tokens, all_down.reshape(adapter_table * 3 * ADAPTER_RANK, model_width)
        ),
        adapter_selector,
        3 * ADAPTER_RANK,
    ).astype(jnp.bfloat16)
    q_delta = jnp.dot(
        spread(adapter_selector, lowrank_part[:, :ADAPTER_RANK]),
        all_up_query.reshape(adapter_table * ADAPTER_RANK, q_width),
        preferred_element_type=jnp.float32,
    )
    k_delta = jnp.dot(
        spread(adapter_selector, lowrank_part[:, ADAPTER_RANK : 2 * ADAPTER_RANK]),
        all_up_keyval[:, :, :kv_width].reshape(adapter_table * ADAPTER_RANK, kv_width),
        preferred_element_type=jnp.float32,
    )
    v_delta = jnp.dot(
        spread(adapter_selector, lowrank_part[:, 2 * ADAPTER_RANK :]),
        all_up_keyval[:, :, kv_width:].reshape(adapter_table * ADAPTER_RANK, kv_width),
        preferred_element_type=jnp.float32,
    )
    queries = rotate(
        (query_base_rows.astype(jnp.float32) + q_delta).reshape(tok_rows, kv_heads * groups, HD),
        positions,
    )
    queries = queries.astype(jnp.bfloat16).reshape(tok_rows, kv_heads, groups, HD)
    key_rows = rotate(
        (key_base_rows.astype(jnp.float32) + k_delta).reshape(tok_rows, kv_heads, HD), positions
    )
    key_rows = key_rows.astype(jnp.bfloat16).reshape(tok_rows, kv_width)
    value_rows = (value_base_rows.astype(jnp.float32) + v_delta).astype(jnp.bfloat16)
    sink_grid = sinks.reshape(kv_heads, groups)
    running_max = jnp.broadcast_to(sink_grid[:, :, None], (kv_heads, groups, tok_rows))
    running_sum = jnp.ones((kv_heads, groups, tok_rows), jnp.float32)
    weighted = jnp.zeros((kv_heads, groups, tok_rows, HD), jnp.float32)
    piece_kv = lax.all_gather(
        jnp.concatenate([key_rows, value_rows], axis=1), "expert", axis=0, tiled=True
    )
    piece_rows = piece_kv.shape[0]
    piece_keys = piece_kv[:, :kv_width].reshape(piece_rows, kv_heads, HD)
    piece_values = piece_kv[:, kv_width:].reshape(piece_rows, kv_heads, HD)
    gate_up_local = jnp.transpose(expert_gate_up_weight[0], (1, 0, 2))
    window = min(piece_rows, piece_rows // 2 + tok_rows)
    window_start = jnp.clip(
        (lax.axis_index("expert") + 1) * tok_rows - window, 0, piece_rows - window
    )
    piece_keys = lax.dynamic_slice_in_dim(piece_keys, window_start, window, 0)
    piece_values = lax.dynamic_slice_in_dim(piece_values, window_start, window, 0)
    window_ids = lax.dynamic_slice_in_dim(row_ids, window_start, window, 0)
    key_index = window_start + jnp.arange(window, dtype=jnp.int32)
    scores = (
        jnp.einsum("tkgd,nkd->kgtn", queries, piece_keys, preferred_element_type=jnp.float32)
        * SCORE_SCALE
    )
    allowed = (key_index[None, :] <= query_index[:, None]) & (
        window_ids[None, :] == my_ids[:, None]
    )
    scores = jnp.where(allowed[None, None], scores, NEGATIVE)
    fresh_max = jnp.maximum(running_max, jnp.max(scores, axis=-1))
    exps = jnp.exp(scores - fresh_max[..., None])
    factor = jnp.exp(running_max - fresh_max)
    running_sum = running_sum * factor + jnp.sum(exps, axis=-1)
    weighted = weighted * factor[..., None] + jnp.einsum(
        "kgtn,nkd->kgtd",
        exps.astype(jnp.bfloat16),
        piece_values,
        preferred_element_type=jnp.float32,
    )
    attended = (
        jnp.transpose(weighted / running_sum[..., None], (2, 0, 1, 3))
        .reshape(tok_rows, q_width)
        .astype(jnp.bfloat16)
    )
    _, expert_blocks = gather_expert_blocks(gate_up_local, down_local)
    o_low = select_adapter(
        multiply_rows(attended, all_o_down.reshape(adapter_table * ADAPTER_RANK, q_width)),
        adapter_selector,
        ADAPTER_RANK,
    ).astype(jnp.bfloat16)
    projected = jnp.dot(attended, attention_output_weight, preferred_element_type=jnp.float32)
    projected = projected + jnp.dot(
        spread(adapter_selector, o_low),
        all_o_up.reshape(adapter_table * ADAPTER_RANK, model_width),
        preferred_element_type=jnp.float32,
    )
    mid = (hidden.astype(jnp.float32) + projected).astype(jnp.bfloat16)
    moe_in = rms_scale(mid, expert_norm_gain)
    exp_dev = expert_gate_up_weight.shape[0]
    experts = lax.axis_size("expert") * exp_dev
    capacity = 5 * tok_rows * TOP // (4 * experts)
    flat_routes = routes.reshape(tok_rows * TOP)
    route_hot = (flat_routes[:, None] == jnp.arange(experts, dtype=jnp.int32)[None, :]).astype(
        jnp.int32
    )
    before = jnp.cumsum(route_hot, axis=0) - route_hot
    slot_index = jnp.sum(before * route_hot, axis=1)
    slot_hot = (
        slot_index[:, None] == jnp.arange(capacity, dtype=jnp.int32)[None, :]
    ).astype(jnp.float32)
    pair_hot = route_hot.astype(jnp.float32)[:, :, None] * slot_hot[:, None, :]
    pair_hot = pair_hot.reshape(tok_rows, TOP, experts, capacity)
    dispatch_hot = jnp.sum(pair_hot, axis=1).astype(jnp.bfloat16)
    dispatch = jnp.einsum(
        "tes,td->esd", dispatch_hot, moe_in, preferred_element_type=jnp.float32
    ).astype(jnp.bfloat16)
    combine = jnp.sum(
        pair_hot * routing_gate_weight[:, :, None, None], axis=1
    )
    arrived = lax.all_to_all(dispatch, "expert", split_axis=0, concat_axis=0, tiled=True)
    summed = jnp.zeros(arrived.shape, jnp.float32)
    for gate_w, up_w, down_ws in expert_blocks:
        gate_out = jnp.einsum("esd,fd->esf", arrived, gate_w, preferred_element_type=jnp.float32)
        up_out = jnp.einsum("esd,fd->esf", arrived, up_w, preferred_element_type=jnp.float32)
        activation = (jax.nn.silu(gate_out) * up_out).astype(jnp.bfloat16)
        part = jnp.zeros(arrived.shape, jnp.float32)
        offset = 0
        for down_w in down_ws:
            part = part + jnp.einsum(
                "esf,fd->esd",
                activation[:, :, offset : offset + down_w.shape[0]],
                down_w,
                preferred_element_type=jnp.float32,
            )
            offset += down_w.shape[0]
        summed = summed + part.astype(jnp.bfloat16).astype(jnp.float32)
    expert_rows = summed.astype(jnp.bfloat16)
    returned = lax.all_to_all(expert_rows, "expert", split_axis=0, concat_axis=0, tiled=True)
    moe = jnp.einsum(
        "tes,esd->td",
        combine,
        returned.astype(jnp.float32),
        precision=lax.Precision.HIGHEST,
        preferred_element_type=jnp.float32,
    )
    return (mid.astype(jnp.float32) + moe).astype(jnp.bfloat16)


def solution(mesh):
    placed = (
        P(("dp", "expert"), None),
        P(("dp", "expert"), None),
        P(("dp", "expert"), None),
        P(("dp", "expert"), None),
        P("dp", "expert"),
        P("dp", None),
        P(),
        P(),
        P("dp", None, None),
        P("dp", None, None),
        P("dp", None, None),
        P("dp", None, None),
        P("dp", None, None),
        P(),
        P(),
        P("expert", "dp", None, None),
        P("expert", "dp", None),
        P(("dp", "expert"), None),
        P(("dp", "expert"), None),
    )

    return jax.shard_map(
        shards, mesh=mesh, in_specs=placed, out_specs=P(("dp", "expert"), None), check_vma=False
    )
```
